768 devices in a mesh: dp: 48 (over y_lo, z, core), section: 4 (over y_hi), mp: 4 (over x).
Axes of the slice: x: 4, y: 8 (y_hi: 4, y_lo: 2; y = y_hi * 2 + y_lo), z: 12, core: 2. Of those that a mesh axis runs over, the one named last changes fastest.
Arguments:
- feature_bank: bfloat16 [12288, 1152], P('dp'), may hold values from -6 to 6
- feature_scale: float32 [48, 9], P('dp'), may hold values from 0.25 to 4
- shard_owner: int32 [48], replicated, may hold values from 0 to 47, each once
- image_shard: int32 [6144, 1], P('dp'), may hold values from 0 to 47; in each aligned block of 128 rows (0 to 127, 128 to 255, ...) at most 5 rows name the same one
- image_row: int32 [6144], P('dp'), may hold values from 0 to 255
- text_doc: int32 [48, 1024], P('dp'), may hold values from 0 to 7, never falling along the last dimension, each value on 1 to 512 neighbouring positions
- image_count: int32 [48, 8], P('dp'), may hold values from 1 to 64, 128 in all within a row
- proj_weight: bfloat16 [1152, 8192], P(None, ('section', 'mp')), may hold values from -0.1875 to 0.1875
- kv_weight: bfloat16 [32768, 1024], P('section', 'mp'), may hold values from -0.0625 to 0.0625
- queries: bfloat16 [49152, 16384], P('dp', ('section', 'mp')), may hold values from -48 to 48
- out_grad: bfloat16 [49152, 16384], P('dp', ('section', 'mp')), may hold values from -0.375 to 0.375
Outputs:
- proj_grad: float32 [1152, 8192], P('dp', ('section', 'mp'))
The draws below stay inside these ranges and needn't reach their ends.
Inputs may be any that keep to these rules, and one draw needn't show every extreme that they name: `image_shard`: the 128 image tokens of one data group name no shard more than 5 times. `shard_owner`: each dp index once. `text_doc`: never falls along a sequence; each of the 8 documents has at least one token. `image_count`: the 8 counts of a data group sum to 128.
All inputs are finite; a program needn't handle non-finite values.
Results may differ from the reference program's by a relative error of at most 0.0085.
Values may be sent and summed in bfloat16 or wider, within the bound.
A program may use at most 64 MiB of HBM per device.

```python
import math
import jax
import jax.numpy as jnp
import numpy as np
from jax import lax

D = 8192
VIS = 1152
HD = 128
GROUP = 8
QBLK = 128
TOK = 1024
IMG = 128
BANK = 256
DOCS = 8
KVH = 4
QH = 32
NBLK = 9
CAP = 5
TOKENS = 49152
N_DP = 48
N_SECTION = 4


def draw_queries(key, part):
    head_count = N_SECTION * QH
    base_key = jax.random.fold_in(key, 101)
    token_key = jax.random.fold_in(key, 202)
    level_key = jax.random.fold_in(key, 303)
    base_values = jnp.clip(jax.random.normal(base_key, (N_DP, TOK, head_count, HD), jnp.float32), -6.0, 6.0)
    picked_token = jax.random.randint(token_key, (N_DP, head_count), 0, TOK)
    level_index = jax.random.randint(level_key, (N_DP, head_count), 0, 3)
    strength_table = jnp.array([3.0, 4.5, 6.0], jnp.float32)
    strength = jnp.take(strength_table, level_index)
    token_ids = jnp.arange(TOK, dtype=jnp.int32)
    marked = token_ids[None, :, None] == picked_token[:, None, :]
    factor = jnp.where(marked, strength[:, None, :], 1.0)
    boosted = jnp.clip(base_values * factor[:, :, :, None], -48.0, 48.0)
    return boosted.reshape(N_DP * TOK, head_count * HD).astype(jnp.bfloat16)


def plant(entries, own_key, least, top_value):
    dims = entries.shape
    index_at = [jax.random.randint(jax.random.fold_in(own_key, axis), (), 0, dims[axis]) for axis in range(len(dims))]
    entries = entries.at[tuple(index_at)].set(least)
    longest = dims.index(max(dims))
    index_at[longest] = (index_at[longest] + 1) % dims[longest]
    return entries.at[tuple(index_at)].set(top_value)


def shard_levels(key, shape, split, smallest, top_value):
    level, own = 1.0, jax.random.fold_in(key, 6)
    for position, shards_of in split:
        draws = jnp.exp(jax.random.uniform(jax.random.fold_in(own, position), (shards_of,), jnp.float32, smallest / len(split), top_value / len(split)))
        level = level * jnp.repeat(draws, shape[position] // shards_of).reshape([-1 if axis == position else 1 for axis in range(len(shape))])
    return level


def profile(count, total, bound, skew):
    weights = [(1 << 20) // math.isqrt(rank ** skew) + 1 for rank in range(2, count + 1)]
    rest, counts = total - bound - (count - 1), [1] * (count - 1)
    while rest > 0:
        movable = [i for i in range(count - 1) if counts[i] < bound]
        pool, budget = sum([weights[i] for i in movable]), rest
        for i in movable:
            more = min(bound - counts[i], max(1, budget * weights[i] // pool), rest)
            counts[i] = counts[i] + more
            rest = rest - more
    return np.array([bound] + counts)


def uneven(stream_key, count, total, most, skew):
    if count == 2:
        one = jax.random.randint(stream_key, (), max(1, total - most), min(most, total - 1) + 1)
        return jnp.stack([one, total - one])
    tallies = jnp.asarray(profile(count, total, most, skew), jnp.int32)
    pairs = (count - 1) // 2
    giver, taker = tallies[1:1 + 2 * pairs:2], tallies[2:2 + 2 * pairs:2]
    margin = jnp.minimum(giver - 1, most - taker)
    moved = jax.random.randint(jax.random.fold_in(stream_key, 1), (pairs,), 0, 1 << 20) % (margin + 1)
    tallies = tallies.at[1:1 + 2 * pairs:2].set(giver - moved).at[2:2 + 2 * pairs:2].set(taker + moved)
    return tallies[jax.random.permutation(jax.random.fold_in(stream_key, 2), count)]


def shared_out(key, own, number, rows, number_of, top, bound, skew):
    ranking = jax.random.permutation(key, number_of)
    crowded, common = portions_of(number_of, rows * top, bound, skew, True), portions_of(number_of, rows * top, bound, skew, False)
    places = jnp.arange(number_of)

    def named(tallies, turn):
        used = int((tallies > 0).sum())
        fixed = max(1, used // 4)
        passed = fixed + (places - fixed + turn * (used - fixed)) % max(1, number_of - fixed)
        return jnp.zeros((number_of,), jnp.int32).at[ranking[jnp.where(places < fixed, places, passed)]].set(jnp.asarray(tallies, jnp.int32))

    tallies = jnp.where(number % 4 == 0, named(crowded, number // 4), named(common, number - number // 4 - 1))
    mixed = jax.random.permutation(jax.random.fold_in(own, 3), number_of)
    donor, taker = mixed[0:number_of // 2 * 2:2], mixed[1:number_of // 2 * 2:2]
    slack = jnp.minimum(tallies[donor] - 1, bound - tallies[taker]) // 2
    slack = jnp.where((donor == ranking[0]) | (taker == ranking[0]) | (tallies[taker] == 0), 0, jnp.maximum(slack, 0))
    passed = jax.random.randint(jax.random.fold_in(own, 4), (number_of // 2,), 0, 1 << 20) % (slack + 1)
    tallies = tallies.at[donor].add(-passed).at[taker].add(passed)
    members = jnp.searchsorted(jnp.cumsum(tallies), jnp.arange(rows * top), side="right").astype(jnp.int32)
    listing = members.reshape(top, rows).T
    listing = listing[jax.random.permutation(jax.random.fold_in(own, 1), rows)]
    turn = jax.random.randint(jax.random.fold_in(own, 2), (rows, 1), 0, top)
    return jnp.take_along_axis(listing, (jnp.arange(top)[None, :] + turn) % top, axis=1)


def portions_of(count, total, bound, lean, full):
    portions = [(1 << 20) // math.isqrt(standing ** lean) + 1 for standing in range(1, count + 1)]
    largest = bound if full else min(bound, max(-(-total // count), total * portions[0] // sum(portions)))
    least = 1 if total - largest >= count - 1 else 0
    counts, surplus = [largest] + [least] * (count - 1), total - largest - least * (count - 1)
    while surplus > 0:
        candidates = [i for i in range(1, count) if counts[i] < largest] or [i for i in range(1, count) if counts[i] < bound]
        pool, left = sum([portions[i] for i in candidates]), surplus
        for i in candidates:
            addition = min(bound - counts[i], max(1, left * portions[i] // pool), surplus)
            counts[i] = counts[i] + addition
            surplus = surplus - addition
    return np.array(counts)


def noise(stream_key, dims, scale, most, split=(), kind=jnp.bfloat16):
    factor_of = shard_levels(stream_key, dims, split, -0.22, 0.18) if split else 1.0
    values = jax.random.normal(stream_key, dims, jnp.float32) * scale * factor_of
    return jnp.minimum(jnp.maximum(values, -most), most).astype(kind)


def setup_inputs(seed: int = 0) -> dict:
    key_of = jax.random.split(jax.random.key(seed), 12)
    feature_bank = noise(key_of[0], (N_DP * BANK, VIS), 1.0, 6.0, ((0, 48),))
    feature_scale = jnp.clip(jnp.exp(math.log(4.0) - 2.7725887 * jax.random.uniform(key_of[1], (N_DP, NBLK), jnp.float32) ** shard_levels(key_of[1], (N_DP, NBLK), ((0, 48),), -0.2, 0.2)), 0.25, 4.0)
    shard_owner = jax.random.permutation(key_of[2], N_DP).astype(jnp.int32)
    image_shard_keys = jax.random.split(jax.random.fold_in(key_of[3], 1), (N_DP * IMG) // IMG)
    image_shard_turns = jax.random.permutation(jax.random.fold_in(key_of[3], 3), (N_DP * IMG) // IMG)
    image_shard = jax.vmap(lambda own, number: shared_out(jax.random.fold_in(key_of[3], 2), own, number, IMG, N_DP, 1, CAP, 2))(image_shard_keys, image_shard_turns).reshape((N_DP * IMG, 1))
    image_row = plant(jax.random.randint(key_of[4], (N_DP * IMG,), 0, BANK), jax.random.fold_in(key_of[4], 1), 0, BANK - 1).astype(jnp.int32)
    text_doc = jax.vmap(lambda own: jnp.searchsorted(jnp.cumsum(uneven(own, DOCS, TOK, TOK // 2, 1)), jnp.arange(TOK), side="right"))(jax.random.split(key_of[5], N_DP)).reshape((N_DP, TOK)).astype(jnp.int32)
    image_count = jax.vmap(lambda own: uneven(own, DOCS, IMG, IMG // 2, 1))(jax.random.split(key_of[6], N_DP)).reshape((N_DP, DOCS)).astype(jnp.int32)
    proj_weight = noise(key_of[7], (VIS, D), VIS ** -0.5, 0.1875, ((1, 16),))
    kv_weight = noise(key_of[8], (N_SECTION * D, KVH * 2 * HD), D ** -0.5, 0.0625, ((0, 4), (1, 4)))
    queries = draw_queries(jax.random.fold_in(key_of[11], 71), 0)
    out_grad = noise(key_of[10], (TOKENS, N_SECTION * QH * HD), (2.0 / (N_DP * IMG) ** 0.5), 0.375, ((0, 48), (1, 16)))
    return dict(feature_bank=feature_bank, feature_scale=feature_scale, shard_owner=shard_owner, image_shard=image_shard, image_row=image_row, text_doc=text_doc, image_count=image_count, proj_weight=proj_weight, kv_weight=kv_weight, queries=queries, out_grad=out_grad)


def gelu(values):
    inner = 0.7978845608028654 * (values + 0.044715 * values * values * values)
    return 0.5 * values * (1.0 + jnp.tanh(inner))

def gelu_slope(values):
    inner = 0.7978845608028654 * (values + 0.044715 * values * values * values)
    tangent = jnp.tanh(inner)
    return 0.5 * (1.0 + tangent) + 0.5 * values * (1.0 - tangent * tangent) * 0.7978845608028654 * (1.0 + 3.0 * 0.044715 * values * values)

def head_backward(query_heads, grad_heads, key_value, token_doc, image_doc):
    head_size = key_value.shape[-1] // 2
    key_raw = key_value[:, :head_size]
    values_low = key_value[:, head_size:].astype(jnp.bfloat16)
    inv_norm = lax.rsqrt(lax.optimization_barrier(jnp.mean(key_raw * key_raw, axis=-1, keepdims=True)) + 1e-06)
    key_unit = key_raw * inv_norm
    key_low = key_unit.astype(jnp.bfloat16)
    score_scale = head_size ** (-0.5)
    scores = jnp.einsum('tgd,id->gti', query_heads.astype(jnp.float32), key_low.astype(jnp.float32)) * score_scale
    same_doc = (token_doc[:, None] == image_doc[None, :])[None, :, :]
    scores = jnp.where(same_doc, scores, -1e+30)
    row_max = lax.optimization_barrier(jnp.max(scores, axis=-1, keepdims=True))
    raised = jnp.where(same_doc, jnp.exp(scores - row_max), 0.0)
    probs = raised / lax.optimization_barrier(jnp.sum(raised, axis=-1, keepdims=True))
    probs_low = probs.astype(jnp.bfloat16)
    dprobs = jnp.einsum('tgd,id->gti', grad_heads.astype(jnp.float32), values_low.astype(jnp.float32))
    dscores = probs * (dprobs - lax.optimization_barrier(jnp.sum(probs * dprobs, axis=-1, keepdims=True)))
    dscores_low = dscores.astype(jnp.bfloat16)
    dvalues = jnp.einsum('gti,tgd->id', probs_low.astype(jnp.float32), grad_heads.astype(jnp.float32))
    key_grad = jnp.einsum('gti,tgd->id', dscores_low.astype(jnp.float32), query_heads.astype(jnp.float32)) * score_scale
    raw_grad = inv_norm * (key_grad - key_unit * lax.optimization_barrier(jnp.mean(key_grad * key_unit, axis=-1, keepdims=True)))
    return jnp.concatenate([raw_grad, dvalues], axis=-1).astype(jnp.bfloat16)

def group_backward(group_items):
    key_value, query_cols, grad_cols, token_doc, image_doc = group_items
    return jax.vmap(head_backward, in_axes=(1, 1, 1, None, None), out_axes=1)(query_cols, grad_cols, key_value, token_doc, image_doc)

def reference(feature_bank, feature_scale, shard_owner, image_shard, image_row, text_doc, image_count, proj_weight, kv_weight, queries, out_grad):
    owner_dev = shard_owner[image_shard[:, 0]].astype(jnp.int32)
    bank_rows = (owner_dev * BANK + image_row).astype(jnp.int32)
    scale_cols = jnp.repeat(feature_scale, QBLK, axis=1)
    features = (feature_bank[bank_rows].astype(jnp.float32) * scale_cols[owner_dev]).astype(jnp.bfloat16)
    pre_act = jnp.dot(features, proj_weight, preferred_element_type=jnp.float32)
    embedded = gelu(pre_act).astype(jnp.bfloat16)
    doc_ends = jnp.cumsum(image_count, axis=1)
    positions = jnp.arange(IMG, dtype=jnp.int32)
    image_doc = lax.optimization_barrier(jnp.sum((doc_ends[:, None, :] <= positions[None, :, None]).astype(jnp.int32), axis=2)).astype(jnp.int32)
    emb_grad = jnp.zeros((N_DP * IMG, D), jnp.float32)
    width = QH * HD
    for section_index in range(N_SECTION):
        layer_weight = kv_weight[section_index * D:(section_index + 1) * D]
        key_value = jnp.dot(embedded, layer_weight, preferred_element_type=jnp.float32).reshape(N_DP, IMG, KVH, 2 * HD)
        query_cols = queries[:, section_index * width:(section_index + 1) * width].reshape(N_DP, TOK, KVH, GROUP, HD)
        grad_cols = out_grad[:, section_index * width:(section_index + 1) * width].reshape(N_DP, TOK, KVH, GROUP, HD)
        kv_grad = lax.map(group_backward, (key_value, query_cols, grad_cols, text_doc, image_doc))
        emb_grad = emb_grad + jnp.dot(kv_grad.reshape(N_DP * IMG, KVH * 2 * HD), layer_weight.T, preferred_element_type=jnp.float32)
    pre_grad = (emb_grad * gelu_slope(pre_act)).astype(jnp.bfloat16)
    return jnp.dot(features.T, pre_grad, preferred_element_type=jnp.float32)
```

```python
import functools

import jax
import jax.numpy as jnp
from jax import lax
from jax.experimental import pallas as pl
from jax.experimental.pallas import tpu as pltpu
from jax.sharding import PartitionSpec as P

QBLK = 128
RING = 4
STREAMS = ((0, 3, "x"), (3, 6, "x"), (6, 8, "y"))
AXIS = {"x": "mp", "y": "section"}


def gelu(values):
    inner = 0.7978845608028654 * (values + 0.044715 * values * values * values)
    return 0.5 * values * (1.0 + jnp.tanh(inner))


def gelu_slope(values):
    inner = 0.7978845608028654 * (values + 0.044715 * values * values * values)
    tangent = jnp.tanh(inner)
    return 0.5 * (1.0 + tangent) + 0.5 * values * (1.0 - tangent * tangent) * 0.7978845608028654 * (
        1.0 + 3.0 * 0.044715 * values * values
    )


def ring_target(axis, step):
    name = AXIS[axis]
    return {name: lax.rem(lax.axis_index(name) + (step + RING) % RING, RING)}


def weight_rows(ds, dx, width):
    s = lax.rem(lax.axis_index("section") + ds, RING)
    m = lax.rem(lax.axis_index("mp") + dx, RING)
    return pl.multiple_of((s * RING + m) * width, width)


def enter(targets):
    barrier = pltpu.get_barrier_semaphore()
    for target in targets:
        pl.semaphore_signal(barrier, 1, device_id=target, device_id_type=pl.DeviceIdType.MESH)
    return lambda: pl.semaphore_wait(barrier, len(targets))


def remote(src, dst, send_sem, recv_sem, target):
    return pltpu.make_async_remote_copy(
        src_ref=src,
        dst_ref=dst,
        send_sem=send_sem,
        recv_sem=recv_sem,
        device_id=target,
        device_id_type=pl.DeviceIdType.MESH,
    )


def ring_neighbours():
    return [ring_target(a, d) for a in "xy" for d in (1, -1)]


def forward_kernel(feat_ref, proj_ref, w_ref, pre_ref, kv_ref, gat, send_sem, recv_sem):
    images, width = pre_ref.shape
    half = width // 2
    ready = enter(ring_neighbours())
    pre = jnp.dot(feat_ref[...], proj_ref[...], preferred_element_type=jnp.float32)
    pre_ref[...] = pre
    gat[0, 0] = gelu(pre).astype(jnp.bfloat16)
    ready()

    def place(first, i, j):
        return (i, j) if first == "y" else (j, i)

    copies = {}
    started = []

    def send(c, key, number, axis, step, src, dst):
        copy = remote(src, dst, send_sem.at[c, number], recv_sem.at[c, number], ring_target(axis, step))
        copy.start()
        copies[c, key] = copy
        started.append(copy)

    def block(c, i, j, part=None):
        lo, hi, first = streams[c]
        a, b = place(first, i, j)
        cols = slice(None) if part is None else slice(part * half, part * half + half)
        return gat.at[a, b, lo:hi, cols]

    unit = images // 8
    streams = [(a * unit, b * unit, "y" if f == "x" else "x") for a, b, f in STREAMS]
    order = (2, 0, 1)

    def second(c, i):
        lo, hi, first = streams[c]
        other = "x" if first == "y" else "y"
        send(c, ("p", i, 0), 4 + 2 * i, other, 1, block(c, i, 0), block(c, i, 3))
        send(c, ("p", i, 1), 5 + 2 * i, other, -1, block(c, i, 0), block(c, i, 1))

    for c in order:
        first = streams[c][2]
        send(c, ("a", 0), 0, first, 1, block(c, 0, 0), block(c, 3, 0))
        send(c, ("a", 1), 1, first, -1, block(c, 0, 0), block(c, 1, 0))
    for c in order:
        second(c, 0)
    for c in order:
        first = streams[c][2]
        copies[c, ("a", 0)].wait_recv()
        send(c, ("b", 0), 2, first, 1, block(c, 3, 0, 0), block(c, 2, 0, 0))
        copies[c, ("a", 1)].wait_recv()
        send(c, ("b", 1), 3, first, -1, block(c, 1, 0, 1), block(c, 2, 0, 1))
        second(c, 3)
        second(c, 1)
    for c in order:
        copies[c, ("b", 0)].wait_recv()
        copies[c, ("b", 1)].wait_recv()
        second(c, 2)

    def forward(c, i, d):
        lo, hi, first = streams[c]
        other = "x" if first == "y" else "y"
        copies[c, ("p", i, d)].wait_recv()
        source = 3 if d == 0 else 1
        send(c, ("q", i), 12 + i, other, 1 if d == 0 else -1, block(c, i, source), block(c, i, 2))

    for i, d in ((0, 0), (3, 1), (1, 0), (2, 1)):
        for c in order:
            forward(c, i, d)

    def term(ds, dx):
        rows = pl.ds(weight_rows(ds, dx, width), width)
        return jnp.dot(gat[ds, dx], w_ref[rows, :], preferred_element_type=jnp.float32)

    kv = term(0, 0)
    waited = {("p", 0, 0), ("p", 3, 1), ("p", 1, 0), ("p", 2, 1), ("a", 0), ("a", 1), ("b", 0), ("b", 1)}
    for (c, key), copy in copies.items():
        if key not in waited:
            copy.wait_recv()
    for ds in range(RING):
        for dx in range(RING):
            if (ds, dx) != (0, 0):
                kv = kv + term(ds, dx)
    kv_ref[...] = kv
    for copy in started:
        copy.wait_send()


def forward(features, proj_weight, kv_weight):
    images, width = features.shape[0], proj_weight.shape[1]
    return pl.pallas_call(
        forward_kernel,
        out_shape=(
            jax.ShapeDtypeStruct((images, width), jnp.float32),
            jax.ShapeDtypeStruct((images, kv_weight.shape[1]), jnp.float32),
        ),
        in_specs=[pl.BlockSpec(memory_space=pltpu.VMEM)] * 3,
        out_specs=(pl.BlockSpec(memory_space=pltpu.VMEM),) * 2,
        scratch_shapes=[
            pltpu.VMEM((RING, RING, images, width), jnp.bfloat16),
            pltpu.SemaphoreType.DMA((len(STREAMS), 16)),
            pltpu.SemaphoreType.DMA((len(STREAMS), 16)),
        ],
        compiler_params=pltpu.CompilerParams(collective_id=1, has_side_effects=True),
        name="project_and_gather",
    )(features, proj_weight, kv_weight)


def backward_kernel(kvg_ref, w_ref, pre_ref, ft_ref, out_ref, *scratch):
    images, width = pre_ref.shape
    half = width // 2
    rows, depth = out_ref.shape[0], ft_ref.shape[1]
    zs = depth // rows
    part, feat, pgs, sums, zsend, zrecv = scratch[:6]
    bufs = [scratch[6 + 8 * c : 14 + 8 * c] for c in range(len(STREAMS))]
    send_sem, recv_sem, dsend_sem, drecv_sem, zsend_sem, zrecv_sem = scratch[6 + 8 * len(STREAMS) :]
    unit = images // 8
    streams = [(a * unit, b * unit, f) for a, b, f in STREAMS]

    place = lax.axis_index("dp")
    core = lax.rem(place, 2)
    z = lax.rem(place // 2, zs)
    y = place // (2 * zs)

    def dp_device(yy, zz, cc):
        return {"dp": (yy * zs + zz) * 2 + cc}

    core_peer = dp_device(y, z, 1 - core)
    y_peer = dp_device(1 - y, z, core)
    both_peer = dp_device(1 - y, z, 1 - core)
    z_at = [lax.rem(z + dz, zs) for dz in range(zs)]
    z_peers = [dp_device(y, z_at[dz], core) for dz in range(1, zs)]
    ready = enter(ring_neighbours() + [core_peer, y_peer, both_peer] + z_peers)

    def partial(ds, dx):
        block = w_ref[pl.ds(weight_rows(ds, dx, width), width), :]
        part[ds, dx] = lax.dot_general(
            kvg_ref[...], block, (((1,), (1,)), ((), ())), preferred_element_type=jnp.float32
        )

    early = [(2, 2)] + [(ds, 2) for ds in (0, 1, 3)] + [(2, dx) for dx in (0, 1, 3)]
    for ds, dx in early:
        partial(ds, dx)
    copies = {}
    started = []

    def ring_send(c, k, d, axis, src, dst):
        n = 2 * k + d
        copy = remote(src, dst, send_sem.at[c, n], recv_sem.at[c, n], ring_target(axis, 1 if d == 0 else -1))
        copy.start()
        copies[c, k, d] = copy
        started.append(copy)

    def own(c, i, j):
        lo, hi, first = streams[c]
        a, b = (j, i) if first == "x" else (i, j)
        return part.at[a, b, lo:hi, :]

    def step1(c):
        a1s, a1r = bufs[c][:2]
        for d in (0, 1):
            for n in (0, 1):
                a1s[d, n] = own(c, 2, 2 * d + n)[...].astype(jnp.bfloat16)
            ring_send(c, 0, d, streams[c][2], a1s.at[d], a1r.at[d])

    def step2(c):
        a1r, a2s, a2r = bufs[c][1:4]
        for d in (0, 1):
            copies[c, 0, d].wait_recv()
            for j in range(RING):
                value = own(c, 1 if d == 0 else 3, j)[...]
                if j // 2 == d:
                    value = value + a1r[d, j % 2].astype(jnp.float32)
                a2s[d, j] = value.astype(jnp.bfloat16)
            ring_send(c, 1, d, streams[c][2], a2s.at[d], a2r.at[d])

    def step3(c):
        a2r, b1s, b1r = bufs[c][3:6]
        other = "y" if streams[c][2] == "x" else "x"
        for d in (0, 1):
            copies[c, 1, d].wait_recv()
        for j in (2, 1, 3, 0):
            ref = own(c, 0, j)
            ref[...] = ref[...] + a2r[0, j].astype(jnp.float32) + a2r[1, j].astype(jnp.float32)
            if j == 2:
                for d in (0, 1):
                    b1s[d] = ref[:, d * half : (d + 1) * half].astype(jnp.bfloat16)
                    ring_send(c, 2, d, other, b1s.at[d], b1r.at[d])

    def step4(c):
        b1r, b2s, b2r = bufs[c][5:8]
        other = "y" if streams[c][2] == "x" else "x"
        for d in (0, 1):
            copies[c, 2, d].wait_recv()
            ref = own(c, 0, 1 if d == 0 else 3)
            for n in (0, 1):
                value = ref[:, n * half : (n + 1) * half]
                if n == d:
                    value = value + b1r[d].astype(jnp.float32)
                b2s[d, :, n * half : (n + 1) * half] = value.astype(jnp.bfloat16)
            ring_send(c, 3, d, other, b2s.at[d], b2r.at[d])

    def dp_send(c, k, src, dst, target):
        copy = remote(src, dst, dsend_sem.at[c, k], drecv_sem.at[c, k], target)
        copy.start()
        copies["dp", c, k] = copy
        started.append(copy)

    def pg_rows(c, k):
        lo, hi, _ = streams[c]
        return pgs.at[k * images + lo : k * images + hi, :]

    def finish(c):
        lo, hi, _ = streams[c]
        b2r = bufs[c][7]
        for d in (0, 1):
            copies[c, 3, d].wait_recv()
        total = own(c, 0, 0)[...] + b2r[0].astype(jnp.float32) + b2r[1].astype(jnp.float32)
        pg_rows(c, 0)[...] = (total * gelu_slope(pre_ref[lo:hi, :])).astype(jnp.bfloat16)
        dp_send(c, 0, pg_rows(c, 0), pg_rows(c, 2), y_peer)
        dp_send(c, 1, pg_rows(c, 0), pg_rows(c, 1), core_peer)

    def relay(c):
        copies["dp", c, 0].wait_recv()
        dp_send(c, 2, pg_rows(c, 2), pg_rows(c, 3), core_peer)

    ready()
    for c in (2, 0, 1):
        step1(c)
    last = len(STREAMS)
    for k, (yy, cc, target) in enumerate(
        ((y, 1 - core, core_peer), (1 - y, core, y_peer), (1 - y, 1 - core, both_peer))
    ):
        dp_send(
            last, k, ft_ref.at[yy * 2 + cc], feat.at[:, (k + 1) * images : (k + 2) * images], target
        )
    for ds in range(RING):
        for dx in range(RING):
            if (ds, dx) not in early:
                partial(ds, dx)
    feat[:, 0:images] = ft_ref[y * 2 + core]
    step2(0), step2(2), step2(1)
    step3(0), step3(2), step4(0), step4(2), step3(1), finish(2), finish(0), step4(1)
    relay(2), relay(0), finish(1), relay(1)
    for c in range(last):
        copies["dp", c, 1].wait_recv()
        copies["dp", c, 2].wait_recv()
    for k in range(3):
        copies["dp", last, k].wait_recv()
    sums[...] = jnp.dot(feat[...], pgs[...], preferred_element_type=jnp.float32)

    def folded(dz):
        value = sums[pl.ds(pl.multiple_of(z_at[dz] * rows, rows), rows), :]
        return jnp.concatenate([value[:, :half], value[:, half:]], axis=0)

    zcopies = []
    far_first = sorted(range(1, zs), key=lambda dz: -min(dz, zs - dz))
    for dz in far_first:
        zsend[dz] = folded(dz).astype(jnp.bfloat16)
        copy = remote(zsend.at[dz], zrecv.at[dz], zsend_sem.at[dz], zrecv_sem.at[dz], z_peers[dz - 1])
        copy.start()
        zcopies.append(copy)
        started.append(copy)
    total = folded(0)
    for dz, copy in sorted(zip(far_first, zcopies), key=lambda item: min(item[0], zs - item[0])):
        copy.wait_recv()
        total = total + zrecv[dz].astype(jnp.float32)
    out_ref[:, :half] = total[:rows]
    out_ref[:, half:] = total[rows:]
    for copy in started:
        copy.wait_send()


def backward(kv_grad, kv_weight, pre_act, feature_rows):
    images, width = pre_act.shape
    depth = feature_rows.shape[1]
    groups = lax.axis_size("dp")
    rows = 4 * depth // groups
    zs = depth // rows
    half = width // 2
    unit = images // 8
    bf16 = jnp.bfloat16
    ring_bufs = []
    for a, b, _ in STREAMS:
        n = (b - a) * unit
        ring_bufs += [pltpu.VMEM((2, 2, n, width), bf16)] * 2
        ring_bufs += [pltpu.VMEM((2, RING, n, width), bf16)] * 2
        ring_bufs += [pltpu.VMEM((2, n, half), bf16)] * 2
        ring_bufs += [pltpu.VMEM((2, n, width), bf16)] * 2
    return pl.pallas_call(
        backward_kernel,
        out_shape=jax.ShapeDtypeStruct((rows, width), jnp.float32),
        in_specs=[pl.BlockSpec(memory_space=pltpu.VMEM)] * 4,
        out_specs=pl.BlockSpec(memory_space=pltpu.VMEM),
        scratch_shapes=[
            pltpu.VMEM((RING, RING, images, width), jnp.float32),
            pltpu.VMEM((depth, 4 * images), bf16),
            pltpu.VMEM((4 * images, width), bf16),
            pltpu.VMEM((depth, width), jnp.float32),
            pltpu.VMEM((zs, 2 * rows, half), bf16),
            pltpu.VMEM((zs, 2 * rows, half), bf16),
            *ring_bufs,
            pltpu.SemaphoreType.DMA((len(STREAMS), 8)),
            pltpu.SemaphoreType.DMA((len(STREAMS), 8)),
            pltpu.SemaphoreType.DMA((len(STREAMS) + 1, 3)),
            pltpu.SemaphoreType.DMA((len(STREAMS) + 1, 3)),
            pltpu.SemaphoreType.DMA((zs,)),
            pltpu.SemaphoreType.DMA((zs,)),
        ],
        compiler_params=pltpu.CompilerParams(collective_id=2, has_side_effects=True),
        name="reduce_gradients",
    )(kv_grad, kv_weight, pre_act, feature_rows)


def feature_rows_of(features):
    images, vis = features.shape
    groups = lax.axis_size("dp")
    zs, rows = groups // 4, vis // groups
    tiles = features.T.reshape(2, zs, 2, rows, images)
    return jnp.moveaxis(tiles, 2, 1).reshape(4, zs * rows, images)


def joined_along(tiles, dim):
    tiles = jnp.moveaxis(tiles, 0, dim)
    dims = tiles.shape
    return tiles.reshape(*dims[:dim], dims[dim] * dims[dim + 1], *dims[dim + 2 :])


def copy_for_each(array, axis):
    peers = lax.axis_size(axis)
    return lax.all_to_all(
        jnp.broadcast_to(array[None], (peers, *array.shape)), axis, 0, 0, tiled=True
    )


def gathered_copies(array, axis, dim):
    return joined_along(copy_for_each(array, axis), dim)


def head_backward(query_heads, grad_heads, key_value, token_doc, image_doc):
    head_size = key_value.shape[-1] // 2
    key_raw = key_value[:, :head_size]
    values_low = key_value[:, head_size:].astype(jnp.bfloat16)
    inv_norm = lax.rsqrt(jnp.mean(key_raw * key_raw, axis=-1, keepdims=True) + 1e-06)
    key_unit = key_raw * inv_norm
    key_low = key_unit.astype(jnp.bfloat16)
    score_scale = head_size ** (-0.5)
    scores = (
        jnp.einsum("tgd,id->gti", query_heads, key_low, preferred_element_type=jnp.float32)
        * score_scale
    )
    same_doc = (token_doc[:, None] == image_doc[None, :])[None, :, :]
    scores = jnp.where(same_doc, scores, -1e30)
    row_max = jnp.max(scores, axis=-1, keepdims=True)
    raised = jnp.where(same_doc, jnp.exp(scores - row_max), 0.0)
    probs = raised / jnp.sum(raised, axis=-1, keepdims=True)
    probs_low = probs.astype(jnp.bfloat16)
    dprobs = jnp.einsum("tgd,id->gti", grad_heads, values_low, preferred_element_type=jnp.float32)
    dscores = probs * (dprobs - jnp.sum(probs * dprobs, axis=-1, keepdims=True))
    dscores_low = dscores.astype(jnp.bfloat16)
    dvalues = jnp.einsum("gti,tgd->id", probs_low, grad_heads, preferred_element_type=jnp.float32)
    key_grad = (
        jnp.einsum("gti,tgd->id", dscores_low, query_heads, preferred_element_type=jnp.float32)
        * score_scale
    )
    raw_grad = inv_norm * (
        key_grad - key_unit * jnp.mean(key_grad * key_unit, axis=-1, keepdims=True)
    )
    return jnp.concatenate([raw_grad, dvalues], axis=-1).astype(jnp.bfloat16)


def body(
    feature_bank,
    feature_scale,
    shard_owner,
    image_shard,
    image_row,
    text_doc,
    image_count,
    proj_weight,
    kv_weight,
    queries,
    out_grad,
):
    groups = lax.axis_size("dp")
    images = image_row.shape[0]
    capacity = max(2, 2 * images // groups)
    owner_dev = shard_owner[image_shard[:, 0]]
    chosen = (owner_dev[:, None] == jnp.arange(groups, dtype=jnp.int32)[None, :]).astype(jnp.int32)
    earlier = jnp.cumsum(chosen, axis=0) - chosen
    slot_index = jnp.sum(earlier * chosen, axis=1)
    wanted = (
        jnp.zeros((groups * capacity,), jnp.int32)
        .at[owner_dev * capacity + slot_index]
        .set(image_row)
    )
    wanted = wanted.reshape(groups, capacity)
    columns = jnp.repeat(feature_scale[0], QBLK)
    slice_width = feature_bank.shape[1] // lax.axis_size(("section", "mp"))
    first_column = lax.axis_index(("section", "mp")) * slice_width
    stored = lax.dynamic_slice_in_dim(feature_bank, first_column, slice_width, 1)
    factors = lax.dynamic_slice_in_dim(columns, first_column, slice_width, 0)
    looked = stored[lax.all_to_all(wanted, "dp", split_axis=0, concat_axis=0, tiled=True)]
    scaled = (looked.astype(jnp.float32) * factors).astype(jnp.bfloat16)
    arrived = lax.all_to_all(scaled, "dp", split_axis=0, concat_axis=0, tiled=True)
    features = arrived[owner_dev, slot_index]
    features = gathered_copies(features, ("section", "mp"), 1)
    pre_act, key_value = forward(features, proj_weight, kv_weight)
    doc_ends = jnp.cumsum(image_count[0])
    positions = jnp.arange(images, dtype=jnp.int32)
    image_doc = jnp.sum((doc_ends[None, :] <= positions[:, None]).astype(jnp.int32), axis=1)
    head_size = kv_weight.shape[1] // 2
    tokens = queries.shape[0]
    query_heads = queries.reshape(tokens, -1, head_size)
    grad_heads = out_grad.reshape(tokens, -1, head_size)
    kv_grad = head_backward(query_heads, grad_heads, key_value, text_doc[0], image_doc)
    return backward(kv_grad, kv_weight, pre_act, feature_rows_of(features))


def solution(mesh):
    placed = (
        P("dp", None),
        P("dp", None),
        P(),
        P("dp", None),
        P("dp"),
        P("dp", None),
        P("dp", None),
        P(None, ("section", "mp")),
        P("section", "mp"),
        P("dp", ("section", "mp")),
        P("dp", ("section", "mp")),
    )
    return jax.shard_map(
        body, mesh=mesh, in_specs=placed, out_specs=P("dp", ("section", "mp")), check_vma=False
    )
```

```python
import functools

import jax
import jax.numpy as jnp
from jax import lax
from jax.experimental import pallas as pl
from jax.experimental.pallas import tpu as pltpu
from jax.sharding import PartitionSpec as P

QBLK = 128
RING = 4
STREAMS = ((0, 3, "x"), (3, 6, "x"), (6, 8, "y"))
AXIS = {"x": "mp", "y": "section"}


def gelu(values):
    inner = 0.7978845608028654 * (values + 0.044715 * values * values * values)
    return 0.5 * values * (1.0 + jnp.tanh(inner))


def gelu_slope(values):
    inner = 0.7978845608028654 * (values + 0.044715 * values * values * values)
    tangent = jnp.tanh(inner)
    return 0.5 * (1.0 + tangent) + 0.5 * values * (1.0 - tangent * tangent) * 0.7978845608028654 * (
        1.0 + 3.0 * 0.044715 * values * values
    )


def ring_target(axis, step):
    name = AXIS[axis]
    return {name: lax.rem(lax.axis_index(name) + (step + RING) % RING, RING)}


def weight_rows(ds, dx, width):
    s = lax.rem(lax.axis_index("section") + ds, RING)
    m = lax.rem(lax.axis_index("mp") + dx, RING)
    return pl.multiple_of((s * RING + m) * width, width)


def enter(targets):
    barrier = pltpu.get_barrier_semaphore()
    for target in targets:
        pl.semaphore_signal(barrier, 1, device_id=target, device_id_type=pl.DeviceIdType.MESH)
    return lambda: pl.semaphore_wait(barrier, len(targets))


def remote(src, dst, send_sem, recv_sem, target):
    return pltpu.make_async_remote_copy(
        src_ref=src,
        dst_ref=dst,
        send_sem=send_sem,
        recv_sem=recv_sem,
        device_id=target,
        device_id_type=pl.DeviceIdType.MESH,
    )


def ring_neighbours():
    return [ring_target(a, d) for a in "xy" for d in (1, -1)]


def forward_kernel(
    owner_ref, shard_ref, row_ref, bank_ref, scale_ref, proj_ref, w_ref,
    pre_ref, kv_ref, feat_ref,
    gat, wsend, wrecv, spread, rsend, rrecv, fgat,
    send_sem, recv_sem, wsend_sem, wrecv_sem, rsend_sem, rrecv_sem, fsend_sem, frecv_sem,
):
    images, width = pre_ref.shape
    half = width // 2
    groups, slots = rsend.shape[:2]
    bank = bank_ref.shape[0]
    blocks = fgat.shape[0]
    here = lax.axis_index("dp")
    member = lax.axis_index("section") * RING + lax.axis_index("mp")
    block_at = lax.rem(member, blocks)
    f32, bf16 = jnp.float32, jnp.bfloat16

    def dp_peer(step):
        return {"dp": lax.rem(here + step, groups)}

    others = [(ds, dx) for ds in range(RING) for dx in range(RING) if ds or dx]

    def other(ds, dx):
        return {**ring_target("y", ds), **ring_target("x", dx)}

    barrier = pltpu.get_barrier_semaphore()

    def greet(step, _):
        pl.semaphore_signal(barrier, 1, device_id=dp_peer(step), device_id_type=pl.DeviceIdType.MESH)
        return 0

    lax.fori_loop(1, groups, greet, 0)
    for ds, dx in others:
        pl.semaphore_signal(barrier, 1, device_id=other(ds, dx), device_id_type=pl.DeviceIdType.MESH)

    def iota(shape, dim):
        return lax.broadcasted_iota(jnp.int32, shape, dim)

    names_shard = (iota((groups, images), 0) == shard_ref[...]).astype(bf16)
    owner = jnp.dot(
        jnp.broadcast_to(owner_ref[...].astype(f32), (8, groups)).astype(bf16),
        names_shard,
        preferred_element_type=f32,
    )[0:1].astype(jnp.int32)
    ahead = owner - here
    ahead = jnp.where(ahead < 0, ahead + groups, ahead)
    chosen = iota((groups, images), 0) == ahead
    chosen_low = chosen.astype(bf16)
    before = (iota((images, images), 0) < iota((images, images), 1)).astype(bf16)
    earlier = jnp.dot(chosen_low, before, preferred_element_type=f32)
    slot = jnp.sum(jnp.where(chosen, earlier, 0.0), axis=0, keepdims=True).astype(jnp.int32)
    row_in_slot = jnp.where(iota((QBLK, images), 0) == slot, row_ref[...], 0).astype(f32).astype(bf16)
    wanted = lax.dot_general(
        chosen_low, row_in_slot, (((1,), (1,)), ((), ())), preferred_element_type=f32
    )
    for step in range(groups):
        wsend[step] = wanted[step : step + 1, :]

    pl.semaphore_wait(barrier, groups - 1 + len(others))

    def request(step):
        return remote(
            wsend.at[step], wrecv.at[step], wsend_sem.at[step], wrecv_sem.at[step], dp_peer(step)
        )

    def answer(step):
        return remote(
            rsend.at[step], rrecv.at[step], rsend_sem.at[step], rrecv_sem.at[step], dp_peer(groups - step)
        )

    def every_step(do):
        def run(step, _):
            do(step)
            return 0

        lax.fori_loop(1, groups, run, 0)

    every_step(lambda step: request(step).start())

    def expand(step, row):
        spread[pl.ds(pl.multiple_of(step * slots, slots), slots), :] = jnp.broadcast_to(row, (slots, QBLK))

    expand(0, wsend[0])

    def received(step):
        request(step).wait_recv()
        expand(step, wrecv[step])

    every_step(received)

    entries = groups * slots
    own_slot = lax.rem(iota((entries, QBLK), 0), slots) == iota((entries, QBLK), 1)
    row = jnp.sum(jnp.where(own_slot, spread[...], 0.0), axis=1, keepdims=True)
    picks = (row == iota((entries, bank), 1).astype(f32)).astype(bf16)
    columns = pl.ds(pl.multiple_of(block_at * QBLK, QBLK), QBLK)
    looked = jnp.dot(picks, bank_ref[:, columns], preferred_element_type=f32)
    scaled = looked * scale_ref[0, block_at]
    rsend[...] = scaled.reshape(groups, slots, QBLK).astype(bf16)

    def block_copy(ds, dx):
        n = ds * RING + dx
        return remote(
            fgat.at[block_at], fgat.at[block_at], fsend_sem.at[n], frecv_sem.at[block_at], other(ds, dx)
        )

    @pl.when(member < blocks)
    def _():
        every_step(lambda step: answer(step).start())
        rrecv[0] = rsend[0]
        at = iota((entries, images), 0)
        selected = (at == ahead * slots + slot).astype(bf16)
        every_step(lambda step: answer(step).wait_recv())
        arrived = rrecv[...].astype(f32).reshape(entries, QBLK).astype(bf16)
        fgat[block_at] = lax.dot_general(
            selected, arrived, (((0,), (0,)), ((), ())), preferred_element_type=f32
        ).astype(bf16)
        for ds, dx in others:
            block_copy(ds, dx).start()

    pre = jnp.zeros((images, width), f32)
    for b in range(blocks):
        @pl.when(member != b)
        def _():
            remote(
                fgat.at[b], fgat.at[b], fsend_sem.at[0], frecv_sem.at[b], other(0, 1)
            ).wait_recv()

        values = fgat[b]
        feat_ref[:, b * QBLK : (b + 1) * QBLK] = values
        pre = pre + jnp.dot(values, proj_ref[b * QBLK : (b + 1) * QBLK, :], preferred_element_type=f32)
    pre_ref[...] = pre
    gat[0, 0] = gelu(pre).astype(bf16)

    def place(first, i, j):
        return (i, j) if first == "y" else (j, i)

    copies = {}
    started = []

    def send(c, key, number, axis, step, src, dst):
        copy = remote(src, dst, send_sem.at[c, number], recv_sem.at[c, number], ring_target(axis, step))
        copy.start()
        copies[c, key] = copy
        started.append(copy)

    def block(c, i, j, part=None):
        lo, hi, first = streams[c]
        a, b = place(first, i, j)
        cols = slice(None) if part is None else slice(part * half, part * half + half)
        return gat.at[a, b, lo:hi, cols]

    unit = images // 8
    streams = [(a * unit, b * unit, "y" if f == "x" else "x") for a, b, f in STREAMS]
    order = (2, 0, 1)

    def second(c, i):
        lo, hi, first = streams[c]
        other = "x" if first == "y" else "y"
        send(c, ("p", i, 0), 4 + 2 * i, other, 1, block(c, i, 0), block(c, i, 3))
        send(c, ("p", i, 1), 5 + 2 * i, other, -1, block(c, i, 0), block(c, i, 1))

    for c in order:
        first = streams[c][2]
        send(c, ("a", 0), 0, first, 1, block(c, 0, 0), block(c, 3, 0))
        send(c, ("a", 1), 1, first, -1, block(c, 0, 0), block(c, 1, 0))
    for c in order:
        second(c, 0)
    for c in order:
        first = streams[c][2]
        copies[c, ("a", 0)].wait_recv()
        send(c, ("b", 0), 2, first, 1, block(c, 3, 0, 0), block(c, 2, 0, 0))
        copies[c, ("a", 1)].wait_recv()
        send(c, ("b", 1), 3, first, -1, block(c, 1, 0, 1), block(c, 2, 0, 1))
        second(c, 3)
        second(c, 1)
    for c in order:
        copies[c, ("b", 0)].wait_recv()
        copies[c, ("b", 1)].wait_recv()
        second(c, 2)

    def forward(c, i, d):
        lo, hi, first = streams[c]
        other = "x" if first == "y" else "y"
        copies[c, ("p", i, d)].wait_recv()
        source = 3 if d == 0 else 1
        send(c, ("q", i), 12 + i, other, 1 if d == 0 else -1, block(c, i, source), block(c, i, 2))

    for i, d in ((0, 0), (3, 1), (1, 0), (2, 1)):
        for c in order:
            forward(c, i, d)

    def term(ds, dx):
        rows = pl.ds(weight_rows(ds, dx, width), width)
        return jnp.dot(gat[ds, dx], w_ref[rows, :], preferred_element_type=jnp.float32)

    kv = term(0, 0)
    waited = {("p", 0, 0), ("p", 3, 1), ("p", 1, 0), ("p", 2, 1), ("a", 0), ("a", 1), ("b", 0), ("b", 1)}
    for (c, key), copy in copies.items():
        if key not in waited:
            copy.wait_recv()
    for ds in range(RING):
        for dx in range(RING):
            if (ds, dx) != (0, 0):
                kv = kv + term(ds, dx)
    kv_ref[...] = kv
    for copy in started:
        copy.wait_send()
    every_step(lambda step: request(step).wait_send())

    @pl.when(member < blocks)
    def _():
        every_step(lambda step: answer(step).wait_send())
        for ds, dx in others:
            block_copy(ds, dx).wait_send()


def forward(shard_owner, image_shard, image_row, feature_bank, feature_scale, proj_weight, kv_weight):
    images, width = image_row.shape[0], proj_weight.shape[1]
    groups, vis = shard_owner.shape[0], proj_weight.shape[0]
    slots = 8
    f32, bf16 = jnp.float32, jnp.bfloat16
    vmem = pl.BlockSpec(memory_space=pltpu.VMEM)
    return pl.pallas_call(
        forward_kernel,
        out_shape=(
            jax.ShapeDtypeStruct((images, width), f32),
            jax.ShapeDtypeStruct((images, kv_weight.shape[1]), f32),
            jax.ShapeDtypeStruct((images, vis), bf16),
        ),
        in_specs=[vmem] * 4 + [pl.BlockSpec(memory_space=pltpu.SMEM)] + [vmem] * 2,
        out_specs=(vmem,) * 3,
        scratch_shapes=[
            pltpu.VMEM((RING, RING, images, width), bf16),
            pltpu.VMEM((groups, 1, QBLK), f32),
            pltpu.VMEM((groups, 1, QBLK), f32),
            pltpu.VMEM((groups * slots, QBLK), f32),
            pltpu.VMEM((groups, slots, QBLK), bf16),
            pltpu.VMEM((groups, slots, QBLK), bf16),
            pltpu.VMEM((vis // QBLK, images, QBLK), bf16),
            pltpu.SemaphoreType.DMA((len(STREAMS), 16)),
            pltpu.SemaphoreType.DMA((len(STREAMS), 16)),
            pltpu.SemaphoreType.DMA((groups,)),
            pltpu.SemaphoreType.DMA((groups,)),
            pltpu.SemaphoreType.DMA((groups,)),
            pltpu.SemaphoreType.DMA((groups,)),
            pltpu.SemaphoreType.DMA((RING * RING,)),
            pltpu.SemaphoreType.DMA((vis // QBLK,)),
        ],
        compiler_params=pltpu.CompilerParams(collective_id=1, has_side_effects=True),
        name="fetch_project_gather",
    )(
        shard_owner.reshape(1, groups),
        image_shard.reshape(1, images),
        image_row.reshape(1, images),
        feature_bank,
        feature_scale,
        proj_weight,
        kv_weight,
    )


def attention(count_ref, doc_ref, kv_ref, q_ref, g_ref, kvg_ref, bias, dk, dv):
    images, head = kv_ref.shape[0], kv_ref.shape[1] // 2
    tokens = q_ref.shape[0]
    chunk = min(tokens, 256)
    f32, bf16 = jnp.float32, jnp.bfloat16
    position = lax.broadcasted_iota(jnp.int32, (images, 1), 0)
    image_doc = jnp.zeros((images, 1), jnp.int32)
    end = 0
    for d in range(count_ref.shape[1]):
        end = end + count_ref[0, d]
        image_doc = image_doc + (end <= position).astype(jnp.int32)
    bias[...] = jnp.where(image_doc == doc_ref[...], 0.0, -1e30)
    key_raw = kv_ref[:, :head]
    values_low = kv_ref[:, head:].astype(bf16)
    inv_norm = lax.rsqrt(jnp.mean(key_raw * key_raw, axis=-1, keepdims=True) + 1e-06)
    key_unit = key_raw * inv_norm
    key_low = key_unit.astype(bf16)
    scale = head ** (-0.5)
    dk[...] = jnp.zeros_like(dk)
    dv[...] = jnp.zeros_like(dv)
    across = (((1,), (1,)), ((), ()))

    def one_head(h, _):
        cols = pl.ds(pl.multiple_of(h * head, head), head)
        for at in range(0, tokens, chunk):
            query = q_ref[at : at + chunk, cols]
            grad = g_ref[at : at + chunk, cols]
            scores = lax.dot_general(key_low, query, across, preferred_element_type=f32) * scale
            scores = scores + bias[:, at : at + chunk]
            raised = jnp.exp(scores - jnp.max(scores, axis=0, keepdims=True))
            probs = raised * (1.0 / jnp.sum(raised, axis=0, keepdims=True))
            dprobs = lax.dot_general(values_low, grad, across, preferred_element_type=f32)
            dscores = probs * (dprobs - jnp.sum(probs * dprobs, axis=0, keepdims=True))
            dv[...] += jnp.dot(probs.astype(bf16), grad, preferred_element_type=f32)
            dk[...] += jnp.dot(dscores.astype(bf16), query, preferred_element_type=f32)
        return 0

    lax.fori_loop(0, q_ref.shape[1] // head, one_head, 0)
    key_grad = dk[...] * scale
    raw_grad = inv_norm * (
        key_grad - key_unit * jnp.mean(key_grad * key_unit, axis=-1, keepdims=True)
    )
    kvg_ref[:, :head] = raw_grad.astype(bf16)
    kvg_ref[:, head:] = dv[...].astype(bf16)


def backward_kernel(
    count_ref, doc_ref, kv_ref, q_ref, g_ref, w_ref, pre_ref, ft_ref, out_ref, bias, kvg_ref, dk, dv, *scratch
):
    images, width = pre_ref.shape
    half = width // 2
    rows, depth = out_ref.shape[0], ft_ref.shape[1]
    zs = depth // rows
    part, feat, pgs, sums, zsend, zrecv = scratch[:6]
    bufs = [scratch[6 + 8 * c : 14 + 8 * c] for c in range(len(STREAMS))]
    send_sem, recv_sem, dsend_sem, drecv_sem, zsend_sem, zrecv_sem = scratch[6 + 8 * len(STREAMS) :]
    unit = images // 8
    streams = [(a * unit, b * unit, f) for a, b, f in STREAMS]

    place = lax.axis_index("dp")
    core = lax.rem(place, 2)
    z = lax.rem(place // 2, zs)
    y = place // (2 * zs)

    def dp_device(yy, zz, cc):
        return {"dp": (yy * zs + zz) * 2 + cc}

    core_peer = dp_device(y, z, 1 - core)
    y_peer = dp_device(1 - y, z, core)
    both_peer = dp_device(1 - y, z, 1 - core)
    z_at = [lax.rem(z + dz, zs) for dz in range(zs)]
    z_peers = [dp_device(y, z_at[dz], core) for dz in range(1, zs)]
    ready = enter(ring_neighbours() + [core_peer, y_peer, both_peer] + z_peers)

    attention(count_ref, doc_ref, kv_ref, q_ref, g_ref, kvg_ref, bias, dk, dv)

    def partial(ds, dx):
        block = w_ref[pl.ds(weight_rows(ds, dx, width), width), :]
        part[ds, dx] = lax.dot_general(
            kvg_ref[...], block, (((1,), (1,)), ((), ())), preferred_element_type=jnp.float32
        )

    early = [(2, 2)] + [(ds, 2) for ds in (0, 1, 3)] + [(2, dx) for dx in (0, 1, 3)]
    for ds, dx in early:
        partial(ds, dx)
    copies = {}
    started = []

    def ring_send(c, k, d, axis, src, dst):
        n = 2 * k + d
        copy = remote(src, dst, send_sem.at[c, n], recv_sem.at[c, n], ring_target(axis, 1 if d == 0 else -1))
        copy.start()
        copies[c, k, d] = copy
        started.append(copy)

    def own(c, i, j):
        lo, hi, first = streams[c]
        a, b = (j, i) if first == "x" else (i, j)
        return part.at[a, b, lo:hi, :]

    def step1(c):
        a1s, a1r = bufs[c][:2]
        for d in (0, 1):
            for n in (0, 1):
                a1s[d, n] = own(c, 2, 2 * d + n)[...].astype(jnp.bfloat16)
            ring_send(c, 0, d, streams[c][2], a1s.at[d], a1r.at[d])

    def step2(c):
        a1r, a2s, a2r = bufs[c][1:4]
        for d in (0, 1):
            copies[c, 0, d].wait_recv()
            for j in range(RING):
                value = own(c, 1 if d == 0 else 3, j)[...]
                if j // 2 == d:
                    value = value + a1r[d, j % 2].astype(jnp.float32)
                a2s[d, j] = value.astype(jnp.bfloat16)
            ring_send(c, 1, d, streams[c][2], a2s.at[d], a2r.at[d])

    def step3(c):
        a2r, b1s, b1r = bufs[c][3:6]
        other = "y" if streams[c][2] == "x" else "x"
        for d in (0, 1):
            copies[c, 1, d].wait_recv()
        for j in (2, 1, 3, 0):
            ref = own(c, 0, j)
            ref[...] = ref[...] + a2r[0, j].astype(jnp.float32) + a2r[1, j].astype(jnp.float32)
            if j == 2:
                for d in (0, 1):
                    b1s[d] = ref[:, d * half : (d + 1) * half].astype(jnp.bfloat16)
                    ring_send(c, 2, d, other, b1s.at[d], b1r.at[d])

    def step4(c):
        b1r, b2s, b2r = bufs[c][5:8]
        other = "y" if streams[c][2] == "x" else "x"
        for d in (0, 1):
            copies[c, 2, d].wait_recv()
            ref = own(c, 0, 1 if d == 0 else 3)
            for n in (0, 1):
                value = ref[:, n * half : (n + 1) * half]
                if n == d:
                    value = value + b1r[d].astype(jnp.float32)
                b2s[d, :, n * half : (n + 1) * half] = value.astype(jnp.bfloat16)
            ring_send(c, 3, d, other, b2s.at[d], b2r.at[d])

    def dp_send(c, k, src, dst, target):
        copy = remote(src, dst, dsend_sem.at[c, k], drecv_sem.at[c, k], target)
        copy.start()
        copies["dp", c, k] = copy
        started.append(copy)

    def pg_rows(c, k):
        lo, hi, _ = streams[c]
        return pgs.at[k * images + lo : k * images + hi, :]

    def finish(c):
        lo, hi, _ = streams[c]
        b2r = bufs[c][7]
        for d in (0, 1):
            copies[c, 3, d].wait_recv()
        total = own(c, 0, 0)[...] + b2r[0].astype(jnp.float32) + b2r[1].astype(jnp.float32)
        pg_rows(c, 0)[...] = (total * gelu_slope(pre_ref[lo:hi, :])).astype(jnp.bfloat16)
        dp_send(c, 0, pg_rows(c, 0), pg_rows(c, 2), y_peer)
        dp_send(c, 1, pg_rows(c, 0), pg_rows(c, 1), core_peer)

    def relay(c):
        copies["dp", c, 0].wait_recv()
        dp_send(c, 2, pg_rows(c, 2), pg_rows(c, 3), core_peer)

    ready()
    for c in (2, 0, 1):
        step1(c)
    last = len(STREAMS)
    for k, (yy, cc, target) in enumerate(
        ((y, 1 - core, core_peer), (1 - y, core, y_peer), (1 - y, 1 - core, both_peer))
    ):
        dp_send(
            last, k, ft_ref.at[yy * 2 + cc], feat.at[:, (k + 1) * images : (k + 2) * images], target
        )
    for ds in range(RING):
        for dx in range(RING):
            if (ds, dx) not in early:
                partial(ds, dx)
    feat[:, 0:images] = ft_ref[y * 2 + core]
    step2(0), step2(2), step2(1)
    step3(0), step3(2), step4(0), step4(2), step3(1), finish(2), finish(0), step4(1)
    relay(2), relay(0), finish(1), relay(1)
    for c in range(last):
        copies["dp", c, 1].wait_recv()
        copies["dp", c, 2].wait_recv()
    for k in range(3):
        copies["dp", last, k].wait_recv()
    sums[...] = jnp.dot(feat[...], pgs[...], preferred_element_type=jnp.float32)

    def folded(dz):
        value = sums[pl.ds(pl.multiple_of(z_at[dz] * rows, rows), rows), :]
        return jnp.concatenate([value[:, :half], value[:, half:]], axis=0)

    zcopies = []
    far_first = sorted(range(1, zs), key=lambda dz: -min(dz, zs - dz))
    for dz in far_first:
        zsend[dz] = folded(dz).astype(jnp.bfloat16)
        copy = remote(zsend.at[dz], zrecv.at[dz], zsend_sem.at[dz], zrecv_sem.at[dz], z_peers[dz - 1])
        copy.start()
        zcopies.append(copy)
        started.append(copy)
    total = folded(0)
    for dz, copy in sorted(zip(far_first, zcopies), key=lambda item: min(item[0], zs - item[0])):
        copy.wait_recv()
        total = total + zrecv[dz].astype(jnp.float32)
    out_ref[:, :half] = total[:rows]
    out_ref[:, half:] = total[rows:]
    for copy in started:
        copy.wait_send()


def backward(image_count, text_doc, key_value, queries, out_grad, kv_weight, pre_act, feature_rows):
    images, width = pre_act.shape
    depth = feature_rows.shape[1]
    groups = lax.axis_size("dp")
    rows = 4 * depth // groups
    zs = depth // rows
    half = width // 2
    unit = images // 8
    bf16 = jnp.bfloat16
    ring_bufs = []
    for a, b, _ in STREAMS:
        n = (b - a) * unit
        ring_bufs += [pltpu.VMEM((2, 2, n, width), bf16)] * 2
        ring_bufs += [pltpu.VMEM((2, RING, n, width), bf16)] * 2
        ring_bufs += [pltpu.VMEM((2, n, half), bf16)] * 2
        ring_bufs += [pltpu.VMEM((2, n, width), bf16)] * 2
    return pl.pallas_call(
        backward_kernel,
        out_shape=jax.ShapeDtypeStruct((rows, width), jnp.float32),
        in_specs=[pl.BlockSpec(memory_space=pltpu.SMEM)] + [pl.BlockSpec(memory_space=pltpu.VMEM)] * 7,
        out_specs=pl.BlockSpec(memory_space=pltpu.VMEM),
        scratch_shapes=[
            pltpu.VMEM((images, text_doc.shape[1]), jnp.float32),
            pltpu.VMEM((images, kv_weight.shape[1]), bf16),
            pltpu.VMEM((images, kv_weight.shape[1] // 2), jnp.float32),
            pltpu.VMEM((images, kv_weight.shape[1] // 2), jnp.float32),
            pltpu.VMEM((RING, RING, images, width), jnp.float32),
            pltpu.VMEM((depth, 4 * images), bf16),
            pltpu.VMEM((4 * images, width), bf16),
            pltpu.VMEM((depth, width), jnp.float32),
            pltpu.VMEM((zs, 2 * rows, half), bf16),
            pltpu.VMEM((zs, 2 * rows, half), bf16),
            *ring_bufs,
            pltpu.SemaphoreType.DMA((len(STREAMS), 8)),
            pltpu.SemaphoreType.DMA((len(STREAMS), 8)),
            pltpu.SemaphoreType.DMA((len(STREAMS) + 1, 3)),
            pltpu.SemaphoreType.DMA((len(STREAMS) + 1, 3)),
            pltpu.SemaphoreType.DMA((zs,)),
            pltpu.SemaphoreType.DMA((zs,)),
        ],
        compiler_params=pltpu.CompilerParams(collective_id=2, has_side_effects=True),
        name="attend_and_reduce",
    )(image_count, text_doc, key_value, queries, out_grad, kv_weight, pre_act, feature_rows)


def feature_rows_of(features):
    images, vis = features.shape
    groups = lax.axis_size("dp")
    zs, rows = groups // 4, vis // groups
    tiles = features.T.reshape(2, zs, 2, rows, images)
    return jnp.moveaxis(tiles, 2, 1).reshape(4, zs * rows, images)


def body(
    feature_bank,
    feature_scale,
    shard_owner,
    image_shard,
    image_row,
    text_doc,
    image_count,
    proj_weight,
    kv_weight,
    queries,
    out_grad,
):
    pre_act, key_value, features = forward(
        shard_owner, image_shard, image_row, feature_bank, feature_scale, proj_weight, kv_weight
    )
    return backward(
        image_count, text_doc, key_value, queries, out_grad, kv_weight, pre_act, feature_rows_of(features)
    )


def solution(mesh):
    placed = (
        P("dp", None),
        P("dp", None),
        P(),
        P("dp", None),
        P("dp"),
        P("dp", None),
        P("dp", None),
        P(None, ("section", "mp")),
        P("section", "mp"),
        P("dp", ("section", "mp")),
        P("dp", ("section", "mp")),
    )
    return jax.shard_map(
        body, mesh=mesh, in_specs=placed, out_specs=P("dp", ("section", "mp")), check_vma=False
    )
```

```python
import jax
import jax.numpy as jnp
from jax import lax
from jax.experimental import pallas as pl
from jax.experimental.pallas import tpu as pltpu
from jax.sharding import PartitionSpec as P

QBLK = 128
RING = 4
SUM_STREAMS = tuple((n, n + 1, "x") for n in range(6)) + ((6, 7, "y"), (7, 8, "y"))
GATHER_STREAMS = ((0, 2, "y"), (2, 4, "y"), (4, 6, "y"), (6, 8, "x"))
AXIS = {"x": "mp", "y": "section"}


def gelu(values):
    inner = 0.7978845608028654 * (values + 0.044715 * values * values * values)
    return 0.5 * values * (1.0 + jnp.tanh(inner))


def gelu_slope(values):
    inner = 0.7978845608028654 * (values + 0.044715 * values * values * values)
    tangent = jnp.tanh(inner)
    return 0.5 * (1.0 + tangent) + 0.5 * values * (1.0 - tangent * tangent) * 0.7978845608028654 * (
        1.0 + 3.0 * 0.044715 * values * values
    )


def ring_target(axis, step):
    name = AXIS[axis]
    return {name: lax.rem(lax.axis_index(name) + (step + RING) % RING, RING)}


def weight_rows(ds, dx, width):
    s = lax.rem(lax.axis_index("section") + ds, RING)
    m = lax.rem(lax.axis_index("mp") + dx, RING)
    return pl.multiple_of((s * RING + m) * width, width)


def remote(src, dst, send_sem, recv_sem, target):
    return pltpu.make_async_remote_copy(
        src_ref=src,
        dst_ref=dst,
        send_sem=send_sem,
        recv_sem=recv_sem,
        device_id=target,
        device_id_type=pl.DeviceIdType.MESH,
    )


def step_kernel(
    owner_ref, shard_ref, row_ref, scale_ref, count_ref, doc_ref,
    bank_hbm, proj_hbm, w_hbm, q_hbm, g_hbm,
    out_ref,
    bank_ref, proj_ref, w_ref, q_ref, g_ref, pre_ref, kv_ref, load_sem,
    gat, wsend, wrecv, spread, rsend, rrecv, fgat,
    send_sem, recv_sem, wsend_sem, wrecv_sem, rsend_sem, rrecv_sem, fsend_sem, frecv_sem,
    *scratch,
):
    loads = [
        pltpu.make_async_copy(src, dst, load_sem.at[n])
        for n, (src, dst) in enumerate(
            ((bank_hbm, bank_ref), (proj_hbm, proj_ref), (w_hbm, w_ref), (q_hbm, q_ref), (g_hbm, g_ref))
        )
    ]
    images, width = pre_ref.shape
    half = width // 2
    groups, slots = rsend.shape[:2]
    bank = bank_ref.shape[0]
    blocks = fgat.shape[0]
    here = lax.axis_index("dp")
    at_s, at_m = lax.axis_index("section"), lax.axis_index("mp")
    is_extra = jnp.logical_and(at_s == 0, at_m == 1)
    holds = jnp.logical_or(lax.rem(at_s + at_m, 2) == 0, is_extra)
    block_at = jnp.where(is_extra, 2 * RING, 2 * at_s + at_m // 2)

    def holder(b):
        return (0, 1) if b == 2 * RING else (b // 2, 2 * (b % 2) + (b // 2) % 2)

    f32, bf16 = jnp.float32, jnp.bfloat16

    def dp_peer(step):
        return {"dp": lax.rem(here + step, groups)}

    others = [(ds, dx) for ds in range(RING) for dx in range(RING) if ds or dx]

    def other(ds, dx):
        return {**ring_target("y", ds), **ring_target("x", dx)}

    barrier = pltpu.get_barrier_semaphore()

    def greet(step, _):
        pl.semaphore_signal(barrier, 1, device_id=dp_peer(step), device_id_type=pl.DeviceIdType.MESH)
        return 0

    lax.fori_loop(1, groups, greet, 0)
    for ds, dx in others:
        pl.semaphore_signal(barrier, 1, device_id=other(ds, dx), device_id_type=pl.DeviceIdType.MESH)
    for load in loads:
        load.start()

    def iota(shape, dim):
        return lax.broadcasted_iota(jnp.int32, shape, dim)

    names_shard = (iota((groups, images), 0) == shard_ref[...]).astype(bf16)
    owner = jnp.dot(
        jnp.broadcast_to(owner_ref[...].astype(f32), (8, groups)).astype(bf16),
        names_shard,
        preferred_element_type=f32,
    )[0:1].astype(jnp.int32)
    ahead = owner - here
    ahead = jnp.where(ahead < 0, ahead + groups, ahead)
    chosen = iota((groups, images), 0) == ahead
    chosen_low = chosen.astype(bf16)
    before = (iota((images, images), 0) < iota((images, images), 1)).astype(bf16)
    earlier = jnp.dot(chosen_low, before, preferred_element_type=f32)
    slot = jnp.sum(jnp.where(chosen, earlier, 0.0), axis=0, keepdims=True).astype(jnp.int32)
    row_in_slot = jnp.where(iota((QBLK, images), 0) == slot, row_ref[...], 0).astype(f32).astype(bf16)
    wanted = lax.dot_general(
        chosen_low, row_in_slot, (((1,), (1,)), ((), ())), preferred_element_type=f32
    )
    for step in range(groups):
        wsend[step] = wanted[step : step + 1, :]

    pl.semaphore_wait(barrier, groups - 1 + len(others))

    def request(step):
        return remote(
            wsend.at[step], wrecv.at[step], wsend_sem.at[step], wrecv_sem.at[step], dp_peer(step)
        )

    def answer(step):
        return remote(
            rsend.at[step], rrecv.at[step], rsend_sem.at[step], rrecv_sem.at[step], dp_peer(groups - step)
        )

    def every_step(do):
        def run(step, _):
            do(step)
            return 0

        lax.fori_loop(1, groups, run, 0)

    every_step(lambda step: request(step).start())

    def expand(step, row):
        spread[pl.ds(pl.multiple_of(step * slots, slots), slots), :] = jnp.broadcast_to(row, (slots, QBLK))

    expand(0, wsend[0])

    def received(step):
        request(step).wait_recv()
        expand(step, wrecv[step])

    every_step(received)

    entries = groups * slots
    own_slot = lax.rem(iota((entries, QBLK), 0), slots) == iota((entries, QBLK), 1)
    row = jnp.sum(jnp.where(own_slot, spread[...], 0.0), axis=1, keepdims=True)
    picks = (row == iota((entries, bank), 1).astype(f32)).astype(bf16)
    loads[0].wait()
    columns = pl.ds(pl.multiple_of(block_at * QBLK, QBLK), QBLK)
    looked = jnp.dot(picks, bank_ref[:, columns], preferred_element_type=f32)
    scaled = looked * scale_ref[0, block_at]
    rsend[...] = scaled.reshape(groups, slots, QBLK).astype(bf16)

    def block_copy(ds, dx):
        n = ds * RING + dx
        return remote(
            fgat.at[block_at], fgat.at[block_at], fsend_sem.at[n], frecv_sem.at[block_at], other(ds, dx)
        )

    @pl.when(holds)
    def _():
        every_step(lambda step: answer(step).start())
        rrecv[0] = rsend[0]
        at = iota((entries, images), 0)
        selected = (at == ahead * slots + slot).astype(bf16)
        every_step(lambda step: answer(step).wait_recv())
        arrived = rrecv[...].astype(f32).reshape(entries, QBLK).astype(bf16)
        fgat[block_at] = lax.dot_general(
            selected, arrived, (((0,), (0,)), ((), ())), preferred_element_type=f32
        ).astype(bf16)
        for ds, dx in others:
            block_copy(ds, dx).start()

    pre = jnp.zeros((images, width), f32)
    loads[1].wait()
    same = (iota((QBLK, QBLK), 0) == iota((QBLK, QBLK), 1)).astype(bf16)
    across = (((1,), (1,)), ((), ()))
    feat_t = scratch[0]
    for b in range(blocks):
        hs, hm = holder(b)

        @pl.when(jnp.logical_or(at_s != hs, at_m != hm))
        def _():
            remote(
                fgat.at[b], fgat.at[b], fsend_sem.at[0], frecv_sem.at[b], other(0, 1)
            ).wait_recv()

        values = fgat[b]
        pre = pre + jnp.dot(values, proj_ref[b * QBLK : (b + 1) * QBLK, :], preferred_element_type=f32)
    pre_ref[...] = pre
    gat[0, 0] = gelu(pre).astype(bf16)

    def place(first, i, j):
        return (i, j) if first == "y" else (j, i)

    copies = {}
    started = []

    def send(c, key, number, axis, step, src, dst):
        copy = remote(src, dst, send_sem.at[c, number], recv_sem.at[c, number], ring_target(axis, step))
        copy.start()
        copies[c, key] = copy
        started.append(copy)

    def block(c, i, j, part=None):
        lo, hi, first = streams[c]
        a, b = place(first, i, j)
        cols = slice(None) if part is None else slice(part * half, part * half + half)
        return gat.at[a, b, lo:hi, cols]

    unit = images // 8
    streams = [(a * unit, b * unit, f) for a, b, f in GATHER_STREAMS]
    order = (3, 0, 1, 2)

    def second(c, i):
        lo, hi, first = streams[c]
        other = "x" if first == "y" else "y"
        send(c, ("p", i, 0), 4 + 2 * i, other, 1, block(c, i, 0), block(c, i, 3))
        send(c, ("p", i, 1), 5 + 2 * i, other, -1, block(c, i, 0), block(c, i, 1))

    for c in order:
        first = streams[c][2]
        send(c, ("a", 0), 0, first, 1, block(c, 0, 0), block(c, 3, 0))
        send(c, ("a", 1), 1, first, -1, block(c, 0, 0), block(c, 1, 0))
    for c in order:
        second(c, 0)
    for c in order:
        first = streams[c][2]
        copies[c, ("a", 0)].wait_recv()
        send(c, ("b", 0), 2, first, 1, block(c, 3, 0, 0), block(c, 2, 0, 0))
        copies[c, ("a", 1)].wait_recv()
        send(c, ("b", 1), 3, first, -1, block(c, 1, 0, 1), block(c, 2, 0, 1))
        second(c, 3)
        second(c, 1)
    for c in order:
        copies[c, ("b", 0)].wait_recv()
        copies[c, ("b", 1)].wait_recv()
        second(c, 2)

    def forward(c, i, d):
        lo, hi, first = streams[c]
        other = "x" if first == "y" else "y"
        copies[c, ("p", i, d)].wait_recv()
        source = 3 if d == 0 else 1
        send(c, ("q", i), 12 + i, other, 1 if d == 0 else -1, block(c, i, source), block(c, i, 2))

    for i, d in ((0, 0), (3, 1), (1, 0), (2, 1)):
        for c in order:
            forward(c, i, d)

    def term(ds, dx):
        rows = pl.ds(weight_rows(ds, dx, width), width)
        return jnp.dot(gat[ds, dx], w_ref[rows, :], preferred_element_type=jnp.float32)

    for b in range(blocks):
        feat_t[b * QBLK : (b + 1) * QBLK, :] = lax.dot_general(
            same, fgat[b], across, preferred_element_type=f32
        ).astype(bf16)
    loads[2].wait()
    kv = term(0, 0)
    waited = {("p", 0, 0), ("p", 3, 1), ("p", 1, 0), ("p", 2, 1), ("a", 0), ("a", 1), ("b", 0), ("b", 1)}
    near = [(ds, dx) for ds in (0, 1, 3) for dx in (0, 1, 3)]
    for (c, key), copy in copies.items():
        if key[0] == "p" and key not in waited:
            copy.wait_recv()
    for ds, dx in near[1:]:
        kv = kv + term(ds, dx)
    for (c, key), copy in copies.items():
        if key[0] == "q":
            copy.wait_recv()
    for ds in range(RING):
        for dx in range(RING):
            if (ds, dx) not in near:
                kv = kv + term(ds, dx)
    kv_ref[...] = kv
    loads[3].wait()
    loads[4].wait()
    reduce_part(count_ref, doc_ref, kv_ref, q_ref, g_ref, w_ref, pre_ref, out_ref, *scratch)
    for copy in started:
        copy.wait_send()
    every_step(lambda step: request(step).wait_send())

    @pl.when(holds)
    def _():
        every_step(lambda step: answer(step).wait_send())
        for ds, dx in others:
            block_copy(ds, dx).wait_send()


def attention(count_ref, doc_ref, kv_ref, q_ref, g_ref, kvg_ref, bias, dk, dv):
    images, head = kv_ref.shape[0], kv_ref.shape[1] // 2
    tokens = q_ref.shape[0]
    chunk = min(tokens, 256)
    f32, bf16 = jnp.float32, jnp.bfloat16
    position = lax.broadcasted_iota(jnp.int32, (images, 1), 0)
    image_doc = jnp.zeros((images, 1), jnp.int32)
    end = 0
    for d in range(count_ref.shape[1]):
        end = end + count_ref[0, d]
        image_doc = image_doc + (end <= position).astype(jnp.int32)
    bias[...] = jnp.where(image_doc == doc_ref[...], 0.0, -1e30)
    key_raw = kv_ref[:, :head]
    values_low = kv_ref[:, head:].astype(bf16)
    inv_norm = lax.rsqrt(jnp.mean(key_raw * key_raw, axis=-1, keepdims=True) + 1e-06)
    key_unit = key_raw * inv_norm
    key_low = key_unit.astype(bf16)
    scale = head ** (-0.5)
    dk[...] = jnp.zeros_like(dk)
    dv[...] = jnp.zeros_like(dv)
    across = (((1,), (1,)), ((), ()))

    def one_head(h, _):
        cols = pl.ds(pl.multiple_of(h * head, head), head)
        for at in range(0, tokens, chunk):
            query = q_ref[at : at + chunk, cols]
            grad = g_ref[at : at + chunk, cols]
            scores = lax.dot_general(key_low, query, across, preferred_element_type=f32) * scale
            scores = scores + bias[:, at : at + chunk]
            raised = jnp.exp(scores - jnp.max(scores, axis=0, keepdims=True))
            probs = raised * (1.0 / jnp.sum(raised, axis=0, keepdims=True))
            dprobs = lax.dot_general(values_low, grad, across, preferred_element_type=f32)
            dscores = probs * (dprobs - jnp.sum(probs * dprobs, axis=0, keepdims=True))
            dv[...] += jnp.dot(probs.astype(bf16), grad, preferred_element_type=f32)
            dk[...] += jnp.dot(dscores.astype(bf16), query, preferred_element_type=f32)
        return 0

    lax.fori_loop(0, q_ref.shape[1] // head, one_head, 0)
    key_grad = dk[...] * scale
    raw_grad = inv_norm * (
        key_grad - key_unit * jnp.mean(key_grad * key_unit, axis=-1, keepdims=True)
    )
    kvg_ref[:, :head] = raw_grad.astype(bf16)
    kvg_ref[:, head:] = dv[...].astype(bf16)


def reduce_part(
    count_ref, doc_ref, kv_ref, q_ref, g_ref, w_ref, pre_ref, out_ref, feat_t, bias, kvg_ref, dk, dv, *scratch
):
    images, width = pre_ref.shape
    half = width // 2
    rows, depth = out_ref.shape[0], feat_t.shape[0] // 2
    zs = depth // (2 * rows)
    part, feat, pgs, sums, zsend, zrecv = scratch[:6]
    bufs = [scratch[6 + 8 * c : 14 + 8 * c] for c in range(len(SUM_STREAMS))]
    send_sem, recv_sem, dsend_sem, drecv_sem, zsend_sem, zrecv_sem = scratch[6 + 8 * len(SUM_STREAMS) :]
    unit = images // 8
    streams = [(a * unit, b * unit, f) for a, b, f in SUM_STREAMS]

    place = lax.axis_index("dp")
    core = lax.rem(place, 2)
    z = lax.rem(place // 2, zs)
    y = place // (2 * zs)

    def dp_device(yy, zz, cc):
        return {"dp": (yy * zs + zz) * 2 + cc}

    core_peer = dp_device(y, z, 1 - core)
    y_peer = dp_device(1 - y, z, core)
    z_at = [lax.rem(z + dz, zs) for dz in range(zs)]
    z_peers = [dp_device(y, z_at[dz], core) for dz in range(1, zs)]

    def partial(ds, dx):
        block = w_ref[pl.ds(weight_rows(ds, dx, width), width), :]
        part[ds, dx] = lax.dot_general(
            kvg_ref[...], block, (((1,), (1,)), ((), ())), preferred_element_type=jnp.float32
        )

    copies = {}
    started = []

    def ring_send(c, k, d, axis, src, dst):
        n = 2 * k + d
        copy = remote(src, dst, send_sem.at[c, n], recv_sem.at[c, n], ring_target(axis, 1 if d == 0 else -1))
        copy.start()
        copies[c, k, d] = copy
        started.append(copy)

    def own(c, i, j):
        lo, hi, first = streams[c]
        a, b = (j, i) if first == "x" else (i, j)
        return part.at[a, b, lo:hi, :]

    def step1(c):
        a1s, a1r = bufs[c][:2]
        for d in (0, 1):
            for n in (0, 1):
                a1s[d, n] = own(c, 2, 2 * d + n)[...].astype(jnp.bfloat16)
            ring_send(c, 0, d, streams[c][2], a1s.at[d], a1r.at[d])

    def step2(c):
        a1r, a2s, a2r = bufs[c][1:4]
        for d in (0, 1):
            copies[c, 0, d].wait_recv()
            for j in range(RING):
                value = own(c, 1 if d == 0 else 3, j)[...]
                if j // 2 == d:
                    value = value + a1r[d, j % 2].astype(jnp.float32)
                a2s[d, j] = value.astype(jnp.bfloat16)
            ring_send(c, 1, d, streams[c][2], a2s.at[d], a2r.at[d])

    def step3(c):
        a2r, b1s, b1r = bufs[c][3:6]
        other = "y" if streams[c][2] == "x" else "x"
        for d in (0, 1):
            copies[c, 1, d].wait_recv()
        for j in (2, 1, 3, 0):
            ref = own(c, 0, j)
            ref[...] = ref[...] + a2r[0, j].astype(jnp.float32) + a2r[1, j].astype(jnp.float32)
            if j == 2:
                for d in (0, 1):
                    b1s[d] = ref[:, d * half : (d + 1) * half].astype(jnp.bfloat16)
                    ring_send(c, 2, d, other, b1s.at[d], b1r.at[d])

    def step4(c):
        b1r, b2s, b2r = bufs[c][5:8]
        other = "y" if streams[c][2] == "x" else "x"
        for d in (0, 1):
            copies[c, 2, d].wait_recv()
            ref = own(c, 0, 1 if d == 0 else 3)
            for n in (0, 1):
                value = ref[:, n * half : (n + 1) * half]
                if n == d:
                    value = value + b1r[d].astype(jnp.float32)
                b2s[d, :, n * half : (n + 1) * half] = value.astype(jnp.bfloat16)
            ring_send(c, 3, d, other, b2s.at[d], b2r.at[d])

    def dp_send(c, k, src, dst, target):
        copy = remote(src, dst, dsend_sem.at[c, k], drecv_sem.at[c, k], target)
        copy.start()
        copies["dp", c, k] = copy
        started.append(copy)

    def pg_rows(c, k):
        lo, hi, _ = streams[c]
        return pgs.at[k * images + lo : k * images + hi, :]

    def finish(c):
        lo, hi, _ = streams[c]
        b2r = bufs[c][7]
        for d in (0, 1):
            copies[c, 3, d].wait_recv()
        total = own(c, 0, 0)[...] + b2r[0].astype(jnp.float32) + b2r[1].astype(jnp.float32)
        pg_rows(c, 0)[...] = (total * gelu_slope(pre_ref[lo:hi, :])).astype(jnp.bfloat16)
        dp_send(c, 0, pg_rows(c, 0), pg_rows(c, 2), y_peer)
        dp_send(c, 1, pg_rows(c, 0), pg_rows(c, 1), core_peer)

    def relay(c):
        copies["dp", c, 0].wait_recv()
        dp_send(c, 2, pg_rows(c, 2), pg_rows(c, 3), core_peer)

    last = len(SUM_STREAMS)

    def y_rows(yy):
        return feat_t.at[pl.ds(pl.multiple_of(yy * depth, depth), depth), :]

    def slot_of(k):
        return feat.at[:, k * images : (k + 1) * images]

    dp_send(last, 0, y_rows(1 - y), slot_of(2), y_peer)
    dp_send(last, 1, y_rows(y), slot_of(1), core_peer)
    slot_of(0)[...] = y_rows(y)[...]
    attention(count_ref, doc_ref, kv_ref, q_ref, g_ref, kvg_ref, bias, dk, dv)
    wide = [c for c in range(last) if streams[c][2] == "x"]
    tall = [c for c in range(last) if streams[c][2] == "y"]
    for ds in (2, 0, 1, 3):
        partial(ds, 2)
    for c in wide:
        step1(c)
    for dx in (0, 1, 3):
        partial(2, dx)
    for c in tall:
        step1(c)
    for dx in (1, 3, 0):
        for ds in (0, 1, 3):
            partial(ds, dx)
    tasks = []
    for n, c in enumerate(wide):
        third = 6 + 1.4 * (n + 1)
        times = (2.5 + 0.7 * n, third, third + 3, third + 6, third + 8.2)
        tasks += [(t, k, c) for k, t in enumerate(times)]
    for n, c in enumerate(tall):
        third = 8 + 2.8 * (n + 1)
        times = (4 + 1.4 * n, third, third + 2.5, third + 5, third + 7.2)
        tasks += [(t, k, c) for k, t in enumerate(times)]
    for _, k, c in sorted(tasks):
        (step2, step3, step4, finish, relay)[k](c)
    copies["dp", last, 0].wait_recv()
    dp_send(last, 2, slot_of(2), slot_of(3), core_peer)
    for c in range(last):
        copies["dp", c, 1].wait_recv()
        copies["dp", c, 2].wait_recv()
    for k in (1, 2):
        copies["dp", last, k].wait_recv()
    sums[...] = jnp.dot(feat[...], pgs[...], preferred_element_type=jnp.float32)

    def folded(dz):
        value = sums[pl.ds(pl.multiple_of((2 * z_at[dz] + core) * rows, rows), rows), :]
        return jnp.concatenate([value[:, :half], value[:, half:]], axis=0)

    zcopies = []
    far_first = sorted(range(1, zs), key=lambda dz: -min(dz, zs - dz))
    for dz in far_first:
        zsend[dz] = folded(dz).astype(jnp.bfloat16)
        copy = remote(zsend.at[dz], zrecv.at[dz], zsend_sem.at[dz], zrecv_sem.at[dz], z_peers[dz - 1])
        copy.start()
        zcopies.append(copy)
        started.append(copy)
    total = folded(0)
    for dz, copy in sorted(zip(far_first, zcopies), key=lambda item: min(item[0], zs - item[0])):
        copy.wait_recv()
        total = total + zrecv[dz].astype(jnp.float32)
    out_ref[:, :half] = total[:rows]
    out_ref[:, half:] = total[rows:]
    for copy in started:
        copy.wait_send()


def body(
    feature_bank,
    feature_scale,
    shard_owner,
    image_shard,
    image_row,
    text_doc,
    image_count,
    proj_weight,
    kv_weight,
    queries,
    out_grad,
):
    images, (vis, width) = image_row.shape[0], proj_weight.shape
    groups, features = shard_owner.shape[0], kv_weight.shape[1]
    rows = vis // groups
    zs, half, unit, slots = groups // 4, width // 2, images // 8, 8
    f32, bf16 = jnp.float32, jnp.bfloat16
    vmem, smem, hbm = (
        pl.BlockSpec(memory_space=space) for space in (pltpu.VMEM, pltpu.SMEM, pl.ANY)
    )
    dma = pltpu.SemaphoreType.DMA
    ring_bufs = []
    for a, b, _ in SUM_STREAMS:
        n = (b - a) * unit
        ring_bufs += [pltpu.VMEM((2, 2, n, width), bf16)] * 2
        ring_bufs += [pltpu.VMEM((2, RING, n, width), bf16)] * 2
        ring_bufs += [pltpu.VMEM((2, n, half), bf16)] * 2
        ring_bufs += [pltpu.VMEM((2, n, width), bf16)] * 2
    large = (feature_bank, proj_weight, kv_weight, queries, out_grad)
    return pl.pallas_call(
        step_kernel,
        out_shape=jax.ShapeDtypeStruct((rows, width), f32),
        in_specs=[vmem] * 3 + [smem] * 2 + [vmem] + [hbm] * 5,
        out_specs=vmem,
        scratch_shapes=[
            *[pltpu.VMEM(array.shape, array.dtype) for array in large],
            pltpu.VMEM((images, width), f32),
            pltpu.VMEM((images, features), f32),
            dma((len(large),)),
            pltpu.VMEM((RING, RING, images, width), bf16),
            pltpu.VMEM((groups, 1, QBLK), f32),
            pltpu.VMEM((groups, 1, QBLK), f32),
            pltpu.VMEM((groups * slots, QBLK), f32),
            pltpu.VMEM((groups, slots, QBLK), bf16),
            pltpu.VMEM((groups, slots, QBLK), bf16),
            pltpu.VMEM((vis // QBLK, images, QBLK), bf16),
            *[dma((len(GATHER_STREAMS), 16))] * 2,
            *[dma((groups,))] * 4,
            dma((RING * RING,)),
            dma((vis // QBLK,)),
            pltpu.VMEM((vis, images), bf16),
            pltpu.VMEM((images, text_doc.shape[1]), f32),
            pltpu.VMEM((images, features), bf16),
            *[pltpu.VMEM((images, features // 2), f32)] * 2,
            pltpu.VMEM((RING, RING, images, width), f32),
            pltpu.VMEM((vis // 2, 4 * images), bf16),
            pltpu.VMEM((4 * images, width), bf16),
            pltpu.VMEM((vis // 2, width), f32),
            *[pltpu.VMEM((zs, 2 * rows, half), bf16)] * 2,
            *ring_bufs,
            *[dma((len(SUM_STREAMS), 8))] * 2,
            *[dma((len(SUM_STREAMS) + 1, 3))] * 2,
            *[dma((zs,))] * 2,
        ],
        compiler_params=pltpu.CompilerParams(collective_id=1, has_side_effects=True),
        name="projector_step",
    )(
        shard_owner.reshape(1, groups),
        image_shard.reshape(1, images),
        image_row.reshape(1, images),
        feature_scale,
        image_count,
        text_doc,
        *large,
    )


def solution(mesh):
    placed = (
        P("dp", None),
        P("dp", None),
        P(),
        P("dp", None),
        P("dp"),
        P("dp", None),
        P("dp", None),
        P(None, ("section", "mp")),
        P("section", "mp"),
        P("dp", ("section", "mp")),
        P("dp", ("section", "mp")),
    )
    return jax.shard_map(
        body, mesh=mesh, in_specs=placed, out_specs=P("dp", ("section", "mp")), check_vma=False
    )
```

```python
import jax
import jax.numpy as jnp
from jax import lax
from jax.experimental import pallas as pl
from jax.experimental.pallas import tpu as pltpu
from jax.sharding import PartitionSpec as P

QBLK = 128
RING = 4
SUM_STREAMS = tuple((n, n + 1, "x") for n in range(6)) + ((6, 7, "y"), (7, 8, "y"))
GATHER_STREAMS = ((0, 2, "y"), (2, 4, "y"), (4, 6, "y"), (6, 8, "x"))
AXIS = {"x": "mp", "y": "section"}


def gelu(values):
    inner = 0.7978845608028654 * (values + 0.044715 * values * values * values)
    return 0.5 * values * (1.0 + jnp.tanh(inner))


def gelu_slope(values):
    inner = 0.7978845608028654 * (values + 0.044715 * values * values * values)
    tangent = jnp.tanh(inner)
    return 0.5 * (1.0 + tangent) + 0.5 * values * (1.0 - tangent * tangent) * 0.7978845608028654 * (
        1.0 + 3.0 * 0.044715 * values * values
    )


def ring_target(axis, step):
    name = AXIS[axis]
    return {name: lax.rem(lax.axis_index(name) + (step + RING) % RING, RING)}


def weight_rows(ds, dx, width):
    s = lax.rem(lax.axis_index("section") + ds, RING)
    m = lax.rem(lax.axis_index("mp") + dx, RING)
    return pl.multiple_of((s * RING + m) * width, width)


def remote(src, dst, send_sem, recv_sem, target):
    return pltpu.make_async_remote_copy(
        src_ref=src,
        dst_ref=dst,
        send_sem=send_sem,
        recv_sem=recv_sem,
        device_id=target,
        device_id_type=pl.DeviceIdType.MESH,
    )


def step_kernel(
    owner_ref, shard_ref, row_ref, scale_ref, count_ref, doc_ref,
    bank_hbm, proj_hbm, w_hbm, q_hbm, g_hbm,
    out_ref,
    bank_ref, proj_ref, w_ref, q_ref, g_ref, pre_ref, kv_ref, load_sem,
    gat, wsend, wrecv, spread, rsend, rrecv, fgat,
    send_sem, recv_sem, wsend_sem, wrecv_sem, rsend_sem, rrecv_sem, fsend_sem, frecv_sem,
    *scratch,
):
    loads = [
        pltpu.make_async_copy(src, dst, load_sem.at[n])
        for n, (src, dst) in enumerate(
            ((bank_hbm, bank_ref), (proj_hbm, proj_ref), (w_hbm, w_ref), (q_hbm, q_ref), (g_hbm, g_ref))
        )
    ]
    images, width = pre_ref.shape
    half = width // 2
    groups, slots = rsend.shape[:2]
    bank = bank_ref.shape[0]
    blocks = fgat.shape[0]
    here = lax.axis_index("dp")
    at_s, at_m = lax.axis_index("section"), lax.axis_index("mp")
    is_extra = jnp.logical_and(at_s == 0, at_m == 1)
    holds = jnp.logical_or(lax.rem(at_s + at_m, 2) == 0, is_extra)
    block_at = jnp.where(is_extra, 2 * RING, 2 * at_s + at_m // 2)

    def holder(b):
        return (0, 1) if b == 2 * RING else (b // 2, 2 * (b % 2) + (b // 2) % 2)

    f32, bf16 = jnp.float32, jnp.bfloat16

    def dp_peer(step):
        return {"dp": lax.rem(here + step, groups)}

    others = [(ds, dx) for ds in range(RING) for dx in range(RING) if ds or dx]

    def other(ds, dx):
        return {**ring_target("y", ds), **ring_target("x", dx)}

    barrier = pltpu.get_barrier_semaphore()

    zs = groups // 4
    far_first = sorted(range(1, groups), key=lambda n: -min(n // 2 % zs, zs - n // 2 % zs))
    for step in far_first:
        pl.semaphore_signal(barrier, 1, device_id=dp_peer(step), device_id_type=pl.DeviceIdType.MESH)
    for ds, dx in others:
        pl.semaphore_signal(barrier, 1, device_id=other(ds, dx), device_id_type=pl.DeviceIdType.MESH)
    for load in loads:
        load.start()

    def iota(shape, dim):
        return lax.broadcasted_iota(jnp.int32, shape, dim)

    names_shard = (iota((groups, images), 0) == shard_ref[...]).astype(bf16)
    owner = jnp.dot(
        jnp.broadcast_to(owner_ref[...].astype(f32), (8, groups)).astype(bf16),
        names_shard,
        preferred_element_type=f32,
    )[0:1].astype(jnp.int32)
    ahead = owner - here
    ahead = jnp.where(ahead < 0, ahead + groups, ahead)
    chosen = iota((groups, images), 0) == ahead
    chosen_low = chosen.astype(bf16)
    before = (iota((images, images), 0) < iota((images, images), 1)).astype(bf16)
    earlier = jnp.dot(chosen_low, before, preferred_element_type=f32)
    slot = jnp.sum(jnp.where(chosen, earlier, 0.0), axis=0, keepdims=True).astype(jnp.int32)
    row_in_slot = jnp.where(iota((QBLK, images), 0) == slot, row_ref[...], 0).astype(f32).astype(bf16)
    wanted = lax.dot_general(
        chosen_low, row_in_slot, (((1,), (1,)), ((), ())), preferred_element_type=f32
    )
    for step in range(groups):
        wsend[step] = wanted[step : step + 1, :]

    pl.semaphore_wait(barrier, groups - 1 + len(others))

    def request(step):
        return remote(
            wsend.at[step], wrecv.at[step], wsend_sem.at[step], wrecv_sem.at[step], dp_peer(step)
        )

    def answer(step):
        return remote(
            rsend.at[step], rrecv.at[step], rsend_sem.at[step], rrecv_sem.at[step], dp_peer(groups - step)
        )

    def every_step(do, order=far_first[::-1]):
        for step in order:
            do(step)

    every_step(lambda step: request(step).start(), far_first)

    def expand(step, row):
        spread[step * slots : (step + 1) * slots, :] = jnp.broadcast_to(row, (slots, QBLK))

    expand(0, wsend[0])

    def received(step):
        request(step).wait_recv()
        expand(step, wrecv[step])

    every_step(received)

    entries = groups * slots
    own_slot = lax.rem(iota((entries, QBLK), 0), slots) == iota((entries, QBLK), 1)
    row = jnp.sum(jnp.where(own_slot, spread[...], 0.0), axis=1, keepdims=True)
    picks = (row == iota((entries, bank), 1).astype(f32)).astype(bf16)
    loads[0].wait()
    columns = pl.ds(pl.multiple_of(block_at * QBLK, QBLK), QBLK)
    looked = jnp.dot(picks, bank_ref[:, columns], preferred_element_type=f32)
    scaled = looked * scale_ref[0, block_at]
    rsend[...] = scaled.reshape(groups, slots, QBLK).astype(bf16)

    def block_copy(ds, dx):
        n = ds * RING + dx
        return remote(
            fgat.at[block_at], fgat.at[block_at], fsend_sem.at[n], frecv_sem.at[block_at], other(ds, dx)
        )

    @pl.when(holds)
    def _():
        every_step(lambda step: answer(step).start(), far_first)
        rrecv[0] = rsend[0]
        at = iota((entries, images), 0)
        selected = (at == ahead * slots + slot).astype(bf16)
        every_step(lambda step: answer(step).wait_recv())
        arrived = rrecv[...].astype(f32).reshape(entries, QBLK).astype(bf16)
        fgat[block_at] = lax.dot_general(
            selected, arrived, (((0,), (0,)), ((), ())), preferred_element_type=f32
        ).astype(bf16)
        for ds, dx in others:
            block_copy(ds, dx).start()

    pre = jnp.zeros((images, width), f32)
    loads[1].wait()
    same = (iota((QBLK, QBLK), 0) == iota((QBLK, QBLK), 1)).astype(bf16)
    across = (((1,), (1,)), ((), ()))
    feat_t = scratch[0]
    for b in range(blocks):
        hs, hm = holder(b)

        @pl.when(jnp.logical_or(at_s != hs, at_m != hm))
        def _():
            remote(
                fgat.at[b], fgat.at[b], fsend_sem.at[0], frecv_sem.at[b], other(0, 1)
            ).wait_recv()

        values = fgat[b]
        pre = pre + jnp.dot(values, proj_ref[b * QBLK : (b + 1) * QBLK, :], preferred_element_type=f32)
    pre_ref[...] = pre
    gat[0, 0] = gelu(pre).astype(bf16)

    def place(first, i, j):
        return (i, j) if first == "y" else (j, i)

    copies = {}
    started = []

    def send(c, key, number, axis, step, src, dst):
        copy = remote(src, dst, send_sem.at[c, number], recv_sem.at[c, number], ring_target(axis, step))
        copy.start()
        copies[c, key] = copy
        started.append(copy)

    def block(c, i, j, part=None):
        lo, hi, first = streams[c]
        a, b = place(first, i, j)
        cols = slice(None) if part is None else slice(part * half, part * half + half)
        return gat.at[a, b, lo:hi, cols]

    unit = images // 8
    streams = [(a * unit, b * unit, f) for a, b, f in GATHER_STREAMS]
    order = (3, 0, 1, 2)

    def second(c, i):
        lo, hi, first = streams[c]
        other = "x" if first == "y" else "y"
        send(c, ("p", i, 0), 4 + 2 * i, other, 1, block(c, i, 0), block(c, i, 3))
        send(c, ("p", i, 1), 5 + 2 * i, other, -1, block(c, i, 0), block(c, i, 1))

    for c in order:
        first = streams[c][2]
        send(c, ("a", 0), 0, first, 1, block(c, 0, 0), block(c, 3, 0))
        send(c, ("a", 1), 1, first, -1, block(c, 0, 0), block(c, 1, 0))
    for c in order:
        second(c, 0)
    for c in order:
        first = streams[c][2]
        copies[c, ("a", 0)].wait_recv()
        send(c, ("b", 0), 2, first, 1, block(c, 3, 0, 0), block(c, 2, 0, 0))
        copies[c, ("a", 1)].wait_recv()
        send(c, ("b", 1), 3, first, -1, block(c, 1, 0, 1), block(c, 2, 0, 1))
        second(c, 3)
        second(c, 1)
    for c in order:
        copies[c, ("b", 0)].wait_recv()
        copies[c, ("b", 1)].wait_recv()
        second(c, 2)

    def forward(c, i, d):
        lo, hi, first = streams[c]
        other = "x" if first == "y" else "y"
        copies[c, ("p", i, d)].wait_recv()
        source = 3 if d == 0 else 1
        send(c, ("q", i), 12 + i, other, 1 if d == 0 else -1, block(c, i, source), block(c, i, 2))

    for i, d in ((0, 0), (3, 1), (1, 0), (2, 1)):
        for c in order:
            forward(c, i, d)

    def term(ds, dx):
        rows = pl.ds(weight_rows(ds, dx, width), width)
        return jnp.dot(gat[ds, dx], w_ref[rows, :], preferred_element_type=jnp.float32)

    for b in range(blocks):
        feat_t[b * QBLK : (b + 1) * QBLK, :] = lax.dot_general(
            same, fgat[b], across, preferred_element_type=f32
        ).astype(bf16)
    loads[2].wait()
    kv = term(0, 0)
    waited = {("p", 0, 0), ("p", 3, 1), ("p", 1, 0), ("p", 2, 1), ("a", 0), ("a", 1), ("b", 0), ("b", 1)}
    near = [(ds, dx) for ds in (0, 1, 3) for dx in (0, 1, 3)]
    for (c, key), copy in copies.items():
        if key[0] == "p" and key not in waited:
            copy.wait_recv()
    for ds, dx in near[1:]:
        kv = kv + term(ds, dx)
    for (c, key), copy in copies.items():
        if key[0] == "q":
            copy.wait_recv()
    for ds in range(RING):
        for dx in range(RING):
            if (ds, dx) not in near:
                kv = kv + term(ds, dx)
    kv_ref[...] = kv
    loads[3].wait()
    loads[4].wait()
    reduce_part(count_ref, doc_ref, kv_ref, q_ref, g_ref, w_ref, pre_ref, out_ref, *scratch)
    for copy in started:
        copy.wait_send()
    every_step(lambda step: request(step).wait_send())

    @pl.when(holds)
    def _():
        every_step(lambda step: answer(step).wait_send())
        for ds, dx in others:
            block_copy(ds, dx).wait_send()


def attention(count_ref, doc_ref, kv_ref, q_ref, g_ref, kvg_ref, bias, dk, dv):
    images, head = kv_ref.shape[0], kv_ref.shape[1] // 2
    tokens = q_ref.shape[0]
    chunk = min(tokens, 1024)
    f32, bf16 = jnp.float32, jnp.bfloat16
    position = lax.broadcasted_iota(jnp.int32, (images, 1), 0)
    image_doc = jnp.zeros((images, 1), jnp.int32)
    end = 0
    for d in range(count_ref.shape[1]):
        end = end + count_ref[0, d]
        image_doc = image_doc + (end <= position).astype(jnp.int32)
    bias[...] = jnp.where(image_doc == doc_ref[...], 0.0, -1e30)
    key_raw = kv_ref[:, :head]
    values_low = kv_ref[:, head:].astype(bf16)
    inv_norm = lax.rsqrt(jnp.mean(key_raw * key_raw, axis=-1, keepdims=True) + 1e-06)
    key_unit = key_raw * inv_norm
    key_low = key_unit.astype(bf16)
    scale = head ** (-0.5)
    dk[...] = jnp.zeros_like(dk)
    dv[...] = jnp.zeros_like(dv)
    across = (((1,), (1,)), ((), ()))

    def one_head(h, _):
        cols = pl.ds(pl.multiple_of(h * head, head), head)
        for at in range(0, tokens, chunk):
            query = q_ref[at : at + chunk, cols]
            grad = g_ref[at : at + chunk, cols]
            scores = lax.dot_general(key_low, query, across, preferred_element_type=f32) * scale
            scores = scores + bias[:, at : at + chunk]
            raised = jnp.exp(scores - jnp.max(scores, axis=0, keepdims=True))
            probs = raised * (1.0 / jnp.sum(raised, axis=0, keepdims=True))
            dprobs = lax.dot_general(values_low, grad, across, preferred_element_type=f32)
            dscores = probs * (dprobs - jnp.sum(probs * dprobs, axis=0, keepdims=True))
            dv[...] += jnp.dot(probs.astype(bf16), grad, preferred_element_type=f32)
            dk[...] += jnp.dot(dscores.astype(bf16), query, preferred_element_type=f32)
        return 0

    lax.fori_loop(0, q_ref.shape[1] // head, one_head, 0, unroll=2)
    key_grad = dk[...] * scale
    raw_grad = inv_norm * (
        key_grad - key_unit * jnp.mean(key_grad * key_unit, axis=-1, keepdims=True)
    )
    kvg_ref[:, :head] = raw_grad.astype(bf16)
    kvg_ref[:, head:] = dv[...].astype(bf16)


def reduce_part(
    count_ref, doc_ref, kv_ref, q_ref, g_ref, w_ref, pre_ref, out_ref, feat_t, bias, kvg_ref, dk, dv, *scratch
):
    images, width = pre_ref.shape
    half = width // 2
    rows, depth = out_ref.shape[0], feat_t.shape[0] // 2
    zs = depth // (2 * rows)
    part, feat, pgs, sums, zsend, zrecv = scratch[:6]
    bufs = [scratch[6 + 8 * c : 14 + 8 * c] for c in range(len(SUM_STREAMS))]
    send_sem, recv_sem, dsend_sem, drecv_sem, zsend_sem, zrecv_sem = scratch[6 + 8 * len(SUM_STREAMS) :]
    unit = images // 8
    streams = [(a * unit, b * unit, f) for a, b, f in SUM_STREAMS]

    place = lax.axis_index("dp")
    core = lax.rem(place, 2)
    z = lax.rem(place // 2, zs)
    y = place // (2 * zs)

    def dp_device(yy, zz, cc):
        return {"dp": (yy * zs + zz) * 2 + cc}

    core_peer = dp_device(y, z, 1 - core)
    y_peer = dp_device(1 - y, z, core)
    z_at = [lax.rem(z + dz, zs) for dz in range(zs)]
    z_peers = [dp_device(y, z_at[dz], core) for dz in range(1, zs)]

    def partial(ds, dx):
        block = w_ref[pl.ds(weight_rows(ds, dx, width), width), :]
        part[ds, dx] = lax.dot_general(
            kvg_ref[...], block, (((1,), (1,)), ((), ())), preferred_element_type=jnp.float32
        )

    copies = {}
    started = []

    def ring_send(c, k, d, axis, src, dst):
        n = 2 * k + d
        copy = remote(src, dst, send_sem.at[c, n], recv_sem.at[c, n], ring_target(axis, 1 if d == 0 else -1))
        copy.start()
        copies[c, k, d] = copy
        started.append(copy)

    def own(c, i, j):
        lo, hi, first = streams[c]
        a, b = (j, i) if first == "x" else (i, j)
        return part.at[a, b, lo:hi, :]

    def step1(c):
        a1s, a1r = bufs[c][:2]
        for d in (0, 1):
            for n in (0, 1):
                a1s[d, n] = own(c, 2, 2 * d + n)[...].astype(jnp.bfloat16)
            ring_send(c, 0, d, streams[c][2], a1s.at[d], a1r.at[d])

    def step2(c):
        a1r, a2s, a2r = bufs[c][1:4]
        for d in (0, 1):
            copies[c, 0, d].wait_recv()
            for j in range(RING):
                value = own(c, 1 if d == 0 else 3, j)[...]
                if j // 2 == d:
                    value = value + a1r[d, j % 2].astype(jnp.float32)
                a2s[d, j] = value.astype(jnp.bfloat16)
            ring_send(c, 1, d, streams[c][2], a2s.at[d], a2r.at[d])

    def step3(c):
        a2r, b1s, b1r = bufs[c][3:6]
        other = "y" if streams[c][2] == "x" else "x"
        for d in (0, 1):
            copies[c, 1, d].wait_recv()
        for j in (2, 1, 3, 0):
            ref = own(c, 0, j)
            ref[...] = ref[...] + a2r[0, j].astype(jnp.float32) + a2r[1, j].astype(jnp.float32)
            if j == 2:
                for d in (0, 1):
                    b1s[d] = ref[:, d * half : (d + 1) * half].astype(jnp.bfloat16)
                    ring_send(c, 2, d, other, b1s.at[d], b1r.at[d])

    def step4(c):
        b1r, b2s, b2r = bufs[c][5:8]
        other = "y" if streams[c][2] == "x" else "x"
        for d in (0, 1):
            copies[c, 2, d].wait_recv()
            ref = own(c, 0, 1 if d == 0 else 3)
            for n in (0, 1):
                value = ref[:, n * half : (n + 1) * half]
                if n == d:
                    value = value + b1r[d].astype(jnp.float32)
                b2s[d, :, n * half : (n + 1) * half] = value.astype(jnp.bfloat16)
            ring_send(c, 3, d, other, b2s.at[d], b2r.at[d])

    def dp_send(c, k, src, dst, target):
        copy = remote(src, dst, dsend_sem.at[c, k], drecv_sem.at[c, k], target)
        copy.start()
        copies["dp", c, k] = copy
        started.append(copy)

    def pg_rows(c, k):
        lo, hi, _ = streams[c]
        return pgs.at[k * images + lo : k * images + hi, :]

    def finish(c):
        lo, hi, _ = streams[c]
        b2r = bufs[c][7]
        for d in (0, 1):
            copies[c, 3, d].wait_recv()
        total = own(c, 0, 0)[...] + b2r[0].astype(jnp.float32) + b2r[1].astype(jnp.float32)
        pg_rows(c, 0)[...] = (total * gelu_slope(pre_ref[lo:hi, :])).astype(jnp.bfloat16)
        dp_send(c, 0, pg_rows(c, 0), pg_rows(c, 2), y_peer)
        dp_send(c, 1, pg_rows(c, 0), pg_rows(c, 1), core_peer)

    def relay(c):
        copies["dp", c, 0].wait_recv()
        dp_send(c, 2, pg_rows(c, 2), pg_rows(c, 3), core_peer)

    last = len(SUM_STREAMS)

    def y_rows(yy):
        return feat_t.at[pl.ds(pl.multiple_of(yy * depth, depth), depth), :]

    def slot_of(k):
        return feat.at[:, k * images : (k + 1) * images]

    dp_send(last, 0, y_rows(1 - y), slot_of(2), y_peer)
    dp_send(last, 1, y_rows(y), slot_of(1), core_peer)
    slot_of(0)[...] = y_rows(y)[...]
    attention(count_ref, doc_ref, kv_ref, q_ref, g_ref, kvg_ref, bias, dk, dv)
    wide = [c for c in range(last) if streams[c][2] == "x"]
    tall = [c for c in range(last) if streams[c][2] == "y"]
    for ds in (2, 0, 1, 3):
        partial(ds, 2)
    for c in wide:
        step1(c)
    for dx in (0, 1, 3):
        partial(2, dx)
    for c in tall:
        step1(c)
    for dx in (1, 3, 0):
        for ds in (0, 1, 3):
            partial(ds, dx)
    tasks = []
    for n, c in enumerate(wide):
        third = 6 + 1.4 * (n + 1)
        times = (2.5 + 0.7 * n, third, third + 3, third + 6, third + 8.2)
        tasks += [(t, k, c) for k, t in enumerate(times)]
    for n, c in enumerate(tall):
        third = 8 + 2.8 * (n + 1)
        times = (4 + 1.4 * n, third, third + 2.5, third + 5, third + 7.2)
        tasks += [(t, k, c) for k, t in enumerate(times)]
    for _, k, c in sorted(tasks):
        (step2, step3, step4, finish, relay)[k](c)
    copies["dp", last, 0].wait_recv()
    dp_send(last, 2, slot_of(2), slot_of(3), core_peer)
    for c in range(last):
        copies["dp", c, 1].wait_recv()
        copies["dp", c, 2].wait_recv()
    for k in (1, 2):
        copies["dp", last, k].wait_recv()
    sums[...] = jnp.dot(feat[...], pgs[...], preferred_element_type=jnp.float32)

    def folded(dz):
        value = sums[pl.ds(pl.multiple_of((2 * z_at[dz] + core) * rows, rows), rows), :]
        return jnp.concatenate([value[:, :half], value[:, half:]], axis=0)

    zcopies = []
    far_first = sorted(range(1, zs), key=lambda dz: -min(dz, zs - dz))
    for dz in far_first:
        zsend[dz] = folded(dz).astype(jnp.bfloat16)
        copy = remote(zsend.at[dz], zrecv.at[dz], zsend_sem.at[dz], zrecv_sem.at[dz], z_peers[dz - 1])
        copy.start()
        zcopies.append(copy)
        started.append(copy)
    total = folded(0)
    for dz, copy in sorted(zip(far_first, zcopies), key=lambda item: min(item[0], zs - item[0])):
        copy.wait_recv()
        total = total + zrecv[dz].astype(jnp.float32)
    out_ref[:, :half] = total[:rows]
    out_ref[:, half:] = total[rows:]
    for copy in started:
        copy.wait_send()


def body(
    feature_bank,
    feature_scale,
    shard_owner,
    image_shard,
    image_row,
    text_doc,
    image_count,
    proj_weight,
    kv_weight,
    queries,
    out_grad,
):
    images, (vis, width) = image_row.shape[0], proj_weight.shape
    groups, features = shard_owner.shape[0], kv_weight.shape[1]
    rows = vis // groups
    zs, half, unit, slots = groups // 4, width // 2, images // 8, 8
    f32, bf16 = jnp.float32, jnp.bfloat16
    vmem, smem, hbm = (
        pl.BlockSpec(memory_space=space) for space in (pltpu.VMEM, pltpu.SMEM, pl.ANY)
    )
    dma = pltpu.SemaphoreType.DMA
    ring_bufs = []
    for a, b, _ in SUM_STREAMS:
        n = (b - a) * unit
        ring_bufs += [pltpu.VMEM((2, 2, n, width), bf16)] * 2
        ring_bufs += [pltpu.VMEM((2, RING, n, width), bf16)] * 2
        ring_bufs += [pltpu.VMEM((2, n, half), bf16)] * 2
        ring_bufs += [pltpu.VMEM((2, n, width), bf16)] * 2
    large = (feature_bank, proj_weight, kv_weight, queries, out_grad)
    return pl.pallas_call(
        step_kernel,
        out_shape=jax.ShapeDtypeStruct((rows, width), f32),
        in_specs=[vmem] * 3 + [smem] * 2 + [vmem] + [hbm] * 5,
        out_specs=vmem,
        scratch_shapes=[
            *[pltpu.VMEM(array.shape, array.dtype) for array in large],
            pltpu.VMEM((images, width), f32),
            pltpu.VMEM((images, features), f32),
            dma((len(large),)),
            pltpu.VMEM((RING, RING, images, width), bf16),
            pltpu.VMEM((groups, 1, QBLK), f32),
            pltpu.VMEM((groups, 1, QBLK), f32),
            pltpu.VMEM((groups * slots, QBLK), f32),
            pltpu.VMEM((groups, slots, QBLK), bf16),
            pltpu.VMEM((groups, slots, QBLK), bf16),
            pltpu.VMEM((vis // QBLK, images, QBLK), bf16),
            *[dma((len(GATHER_STREAMS), 16))] * 2,
            *[dma((groups,))] * 4,
            dma((RING * RING,)),
            dma((vis // QBLK,)),
            pltpu.VMEM((vis, images), bf16),
            pltpu.VMEM((images, text_doc.shape[1]), f32),
            pltpu.VMEM((images, features), bf16),
            *[pltpu.VMEM((images, features // 2), f32)] * 2,
            pltpu.VMEM((RING, RING, images, width), f32),
            pltpu.VMEM((vis // 2, 4 * images), bf16),
            pltpu.VMEM((4 * images, width), bf16),
            pltpu.VMEM((vis // 2, width), f32),
            *[pltpu.VMEM((zs, 2 * rows, half), bf16)] * 2,
            *ring_bufs,
            *[dma((len(SUM_STREAMS), 8))] * 2,
            *[dma((len(SUM_STREAMS) + 1, 3))] * 2,
            *[dma((zs,))] * 2,
        ],
        compiler_params=pltpu.CompilerParams(collective_id=1, has_side_effects=True),
        name="projector_step",
    )(
        shard_owner.reshape(1, groups),
        image_shard.reshape(1, images),
        image_row.reshape(1, images),
        feature_scale,
        image_count,
        text_doc,
        *large,
    )


def solution(mesh):
    placed = (
        P("dp", None),
        P("dp", None),
        P(),
        P("dp", None),
        P("dp"),
        P("dp", None),
        P("dp", None),
        P(None, ("section", "mp")),
        P("section", "mp"),
        P("dp", ("section", "mp")),
        P("dp", ("section", "mp")),
    )
    return jax.shard_map(
        body, mesh=mesh, in_specs=placed, out_specs=P("dp", ("section", "mp")), check_vma=False
    )
```
